512 devices in a mesh: rows: 128 (over z, y_hi, x), feat: 4 (over y_lo, core).
Axes of the slice: x: 4, y: 8 (y_hi: 4, y_lo: 2; y = y_hi * 2 + y_lo), z: 8, core: 2. Of those that a mesh axis runs over, the one named last changes fastest.
Arguments:
- band_feats: float32 [65536, 1024], P('rows', 'feat'), may hold values from -6 to 6
- head_feats: float32 [512, 1024], P('rows', 'feat'), may hold values from -6 to 6
- mix_weights: bfloat16 [2, 1024, 1024], P(None, None, 'feat'), may hold values from -0.1875 to 0.1875
- tile_place: int32 [4096, 3], P('rows'), may hold values from -1 to 3, as said below
- tile_vals: bfloat16 [4096, 128, 128], P('rows'), may hold values from -1 to 1
- arrow_cols: bfloat16 [65536, 512], P('rows'), may hold values from -1 to 1
- arrow_reach: int32 [65536], P('rows'), may hold values from 1 to 512
- arrow_rows: bfloat16 [512, 65536], P(None, 'rows'), may hold values from -0.125 to 0.125
- band_degree: int32 [65536], P('rows'), may hold values from 8 to 32
- head_degree: int32 [512], replicated, may hold values from 8 to 32
Outputs:
- band_out: float32 [65536, 1024], P('rows', 'feat')
- head_out: float32 [512, 1024], P('rows', 'feat')
The draws below stay inside these ranges and needn't reach their ends.
Inputs may be any that keep to these rules, and one draw needn't show every extreme that they name: `tile_place`: row and column lie in 0 to 3 and the offset in -1 to 1; the 32 slots of every block hold offsets -1, 0 and 1.
All inputs are finite; a program needn't handle non-finite values.
Results may differ from the reference program's by a relative error of at most 0.0057.
Values may be sent and summed in bfloat16 or wider, within the bound.
A program may use at most 64 MiB of HBM per device.

```python
import jax
import jax.numpy as jnp
from jax import lax

F = 1024
ARROW = 512
TILE = 128
TPR = 8
ITERS = 2
ROWS_DEV = 512
TPD = 32
NB = 65536


def draw_tile_place(key, part):
    blocks = NB // ROWS_DEV
    tile_rows = ROWS_DEV // TILE
    key_row, key_col, key_off = jax.random.split(key, 3)
    row_pick = jax.random.randint(key_row, (blocks, TPD), 0, tile_rows)
    col_pick = jax.random.randint(key_col, (blocks, TPD), 0, tile_rows)
    off_pick = jax.random.randint(key_off, (blocks, TPD), -1, 2)
    slot = jnp.broadcast_to(jnp.arange(TPD, dtype=jnp.int32)[None, :], (blocks, TPD))
    off_pick = jnp.where(slot == 0, -1, jnp.where(slot == 1, 1, jnp.where(slot == 2, 0, off_pick)))
    row_pick = jnp.where(slot == 2, tile_rows - 1, row_pick)
    col_pick = jnp.where(slot == 2, tile_rows - 1, col_pick)
    stacked = jnp.stack([row_pick, col_pick, off_pick], axis=-1)
    return stacked.reshape(blocks * TPD, 3).astype(jnp.int32)


def with_ends(entries, rng, low, top_value):
    longest = entries.shape.index(max(entries.shape))
    spots = []
    for shift in (0, 1):
        where = [jax.random.randint(jax.random.fold_in(rng, axis), (), 0, length) for axis, length in enumerate(entries.shape)]
        where[longest] = (where[longest] + shift) % entries.shape[longest]
        spots.append(tuple(where))
    return entries.at[spots[0]].set(low).at[spots[1]].set(top_value)


def block_scale(stream_key, dims, shards, least, top_value):
    def one(position, parts):
        heights = jax.random.uniform(jax.random.fold_in(jax.random.fold_in(stream_key, 6), position), (parts,), jnp.float32, least / len(shards), top_value / len(shards))
        return jnp.repeat(jnp.exp(heights), dims[position] // parts).reshape((-1,) + (1,) * (len(dims) - position - 1))

    level = one(*shards[0])
    for cut in shards[1:]:
        level = level * one(*cut)
    return level


def bell_draw(stream_key, shape, spread, reach, pieces=(), kind=jnp.bfloat16):
    drawn = jax.random.normal(stream_key, shape, jnp.float32) * spread
    if len(pieces) > 0:
        drawn = block_scale(stream_key, shape, pieces, -0.22, 0.18) * drawn
    return jnp.clip(drawn, min=-reach, max=reach).astype(kind)


def setup_inputs(seed: int = 0) -> dict:
    key_list = jax.random.split(jax.random.key(seed), 11)
    band_feats = bell_draw(key_list[0], (NB, F), 1.0, 6.0, ((0, 128), (1, 4)), jnp.float32)
    head_feats = bell_draw(key_list[1], (ARROW, F), 1.0, 6.0, ((0, 128), (1, 4)), jnp.float32)
    mix_weights = bell_draw(key_list[2], (ITERS, F, F), F ** -0.5, 0.1875, ((2, 4),))
    tile_place = draw_tile_place(jax.random.fold_in(key_list[10], 71), 0)
    tile_vals = bell_draw(key_list[4], (NB // TILE * TPR, TILE, TILE), ((TPR * TILE + ARROW // 2) // 35) ** -0.5, 1.0, ((0, 128),))
    arrow_cols = bell_draw(key_list[5], (NB, ARROW), ((TPR * TILE + ARROW // 2) // 35) ** -0.5, 1.0, ((0, 128),))
    arrow_reach = with_ends(jax.random.randint(key_list[6], (NB,), 1, ARROW + 1), jax.random.fold_in(key_list[6], 1), 1, ARROW).astype(jnp.int32)
    arrow_rows = bell_draw(key_list[7], (ARROW, NB), (NB // 35) ** -0.5, 0.125, ((1, 128),))
    band_degree = with_ends(jax.random.randint(key_list[8], (NB,), 8, 33), jax.random.fold_in(key_list[8], 1), 8, 32).astype(jnp.int32)
    head_degree = with_ends(jax.random.randint(key_list[9], (ARROW,), 8, 33), jax.random.fold_in(key_list[9], 1), 8, 32).astype(jnp.int32)
    return {"band_feats": band_feats, "head_feats": head_feats, "mix_weights": mix_weights, "tile_place": tile_place, "tile_vals": tile_vals, "arrow_cols": arrow_cols, "arrow_reach": arrow_reach, "arrow_rows": arrow_rows, "band_degree": band_degree, "head_degree": head_degree}


def band_product(band_x, tile_place, tile_vals):
    blocks = NB // ROWS_DEV
    tile_rows = ROWS_DEV // TILE
    padded = jnp.concatenate([jnp.zeros((ROWS_DEV, F), jnp.bfloat16), band_x, jnp.zeros((ROWS_DEV, F), jnp.bfloat16)], axis=0)

    def one_block(inputs):
        block_pos, places, values = inputs
        window = lax.dynamic_slice_in_dim(padded, (block_pos * ROWS_DEV).astype(jnp.int32), 3 * ROWS_DEV, 0)
        window = window.reshape(3 * tile_rows, TILE, F)
        column = (places[:, 2] + 1) * tile_rows + places[:, 1]
        picked = window[column].astype(jnp.float32)
        products = jnp.einsum('sij,sjf->sif', values.astype(jnp.float32), picked, precision=lax.Precision.HIGHEST)
        onehot = (places[:, 0][None, :] == jnp.arange(tile_rows, dtype=jnp.int32)[:, None]).astype(jnp.float32)
        summed = jnp.einsum('rs,sif->rif', onehot, products, precision=lax.Precision.HIGHEST)
        return summed.reshape(ROWS_DEV, F)
    result = lax.map(one_block, (jnp.arange(blocks, dtype=jnp.int32), tile_place.reshape(blocks, TPD, 3), tile_vals.reshape(blocks, TPD, TILE, TILE)))
    return result.reshape(NB, F)

def reference(band_feats, head_feats, mix_weights, tile_place, tile_vals, arrow_cols, arrow_reach, arrow_rows, band_degree, head_degree):
    reach_mask = jnp.arange(ARROW, dtype=jnp.int32)[None, :] < arrow_reach[:, None]
    masked_cols = jnp.where(reach_mask, arrow_cols, jnp.zeros_like(arrow_cols))
    band_scale = lax.rsqrt(band_degree.astype(jnp.float32))[:, None]
    head_scale = lax.rsqrt(head_degree.astype(jnp.float32))[:, None]
    band_state, head_state = (band_feats, head_feats)
    for layer_step in range(ITERS):
        mixing = mix_weights[layer_step]
        band_x = jnp.dot(band_state.astype(jnp.bfloat16), mixing, preferred_element_type=jnp.float32).astype(jnp.bfloat16)
        head_x = jnp.dot(head_state.astype(jnp.bfloat16), mixing, preferred_element_type=jnp.float32).astype(jnp.bfloat16)
        band_sum = band_product(band_x, tile_place, tile_vals) + jnp.dot(masked_cols, head_x, preferred_element_type=jnp.float32)
        head_sum = jnp.dot(arrow_rows, band_x, preferred_element_type=jnp.float32)
        band_state = jnp.maximum(band_sum * band_scale, 0.0)
        head_state = jnp.maximum(head_sum * head_scale, 0.0)
    return (band_state, head_state)
```

```python
import functools

import jax
import jax.numpy as jnp
from jax import lax
from jax.experimental import pallas as pl
from jax.experimental.pallas import tpu as pltpu
from jax.sharding import Mesh
from jax.sharding import PartitionSpec as P

MESH = pl.DeviceIdType.MESH
F32, BF16 = jnp.float32, jnp.bfloat16
NZ, NY, NX, NL, NC = 4, 4, 8, 2, 2
ROWS = ("z", "yh", "x")
FEAT = ("yl", "core")
TILE = 128
CHUNKS = 4


def dot(a, b):
    return jnp.dot(a, b, preferred_element_type=F32)


def down_rows(line):
    return jnp.broadcast_to(line, (TILE, line.shape[-1])).T


def kernel(
    place,
    deg,
    hdeg,
    reach,
    x_hbm,
    h_hbm,
    w_hbm,
    t_hbm,
    c_hbm,
    r_hbm,
    band_out,
    head_out,
    xin,
    hin,
    wts,
    tiles,
    cols,
    rws,
    dense,
    gath,
    win,
    acc,
    part,
    part_b,
    zin,
    ysrc,
    yin,
    xsrc,
    xin_h,
    feat_h,
    h4,
    head,
    hscale,
    bscale,
    cell,
    lsem,
    ssem,
    rsem,
):
    z, yh, x = (lax.axis_index(a) for a in ROWS)
    yl, core = (lax.axis_index(a) for a in FEAT)
    rank = (z * NY + yh) * NX + x
    me_f = yl * NC + core
    rows = xin.shape[0]
    step_rows = rows // CHUNKS
    tile_rows = rows // TILE
    has_left, has_right = rank > 0, rank < NZ * NY * NX - 1

    def at_rank(r):
        return {"z": r // (NY * NX), "yh": (r // NX) % NY, "x": r % NX}

    left = at_rank(jnp.maximum(rank - 1, 0))
    right = at_rank(jnp.minimum(rank + 1, NZ * NY * NX - 1))
    z_peers = [{"z": (z + k) % NZ} for k in range(1, NZ)]
    y_peers = [{"yh": (yh + k) % NY} for k in range(1, NY)]
    x_peers = [{"x": (x + k) % NX} for k in range(1, NX)]
    mate = {"core": 1 - core}
    across = {"yl": 1 - yl}
    f_peers = [mate, across, {"yl": 1 - yl, "core": 1 - core}]
    f_slots = [yl * NC + 1 - core, (1 - yl) * NC + core, (1 - yl) * NC + 1 - core]

    used = [0]
    started = []

    def remote(src, dst, device):
        i = used[0]
        used[0] += 1
        return pltpu.make_async_remote_copy(
            src_ref=src,
            dst_ref=dst,
            send_sem=ssem.at[i],
            recv_sem=rsem.at[i],
            device_id=device,
            device_id_type=MESH,
        )

    def push(src, dst, device):
        copy = remote(src, dst, device)
        copy.start()
        started.append(copy)
        return copy

    barrier = pltpu.get_barrier_semaphore()
    greet = z_peers + y_peers + x_peers + f_peers
    for peer in greet:
        pl.semaphore_signal(barrier, inc=1, device_id=peer, device_id_type=MESH)

    @pl.when(has_left)
    def _():
        pl.semaphore_signal(barrier, inc=1, device_id=left, device_id_type=MESH)

    @pl.when(has_right)
    def _():
        pl.semaphore_signal(barrier, inc=1, device_id=right, device_id_type=MESH)

    loads = []
    for i, (src, dst) in enumerate(
        ((x_hbm, xin), (h_hbm, hin), (r_hbm, rws), (t_hbm, tiles), (w_hbm, wts), (c_hbm, cols))
    ):
        load = pltpu.make_async_copy(src, dst, lsem.at[i])
        load.start()
        loads.append(load)
    load_x, load_h, load_r, load_t, load_w, load_c = loads

    load_h.wait()
    h4[pl.ds(x, 1)] = hin[...][None]
    load_x.wait()
    gath[0, pl.ds(me_f, 1)] = xin[...].astype(BF16)[None]
    load_r.wait()

    def head_partial(step):
        part[...] = dot(rws[...], gath[step, me_f]).reshape(part.shape)
        part_b[step] = part[...].astype(BF16)

    head_partial(0)
    pl.semaphore_wait(
        barrier, len(greet) + has_left.astype(jnp.int32) + has_right.astype(jnp.int32)
    )

    def z_start(step):
        return [
            push(part_b.at[step, (z + k) % NZ], zin.at[step, k - 1], z_peers[k - 1])
            for k in range(1, NZ)
        ]

    def z_finish(step, copies):
        total = part[z]
        for k in range(1, NZ):
            copies[k - 1].wait_recv()
            total = total + zin[step, k - 1].astype(F32)
        ysrc[step] = total.reshape(NY, -1, total.shape[-1])
        return [
            push(ysrc.at[step, (yh + k) % NY], yin.at[step, k - 1], y_peers[k - 1])
            for k in range(1, NY)
        ]

    def y_finish(step, copies):
        total = ysrc[step, yh]
        for k in range(1, NY):
            copies[k - 1].wait_recv()
            total = total + yin[step, k - 1]
        acc_x[0] = total
        xsrc[step] = total.astype(BF16)
        return [
            push(xsrc.at[step], xin_h.at[step, k - 1], x_peers[k - 1]) for k in range(1, NX)
        ]

    acc_x = [None]

    def x_finish(step, copies):
        for copy in copies:
            copy.wait_recv()
        total = xsrc[step].astype(F32)
        for k in range(1, NX):
            total = total + xin_h[step, k - 1].astype(F32)
        return total

    def feat_start(i, value):
        feat_h[i, pl.ds(me_f, 1)] = value.astype(BF16)[None]
        return [push(feat_h.at[i, me_f], feat_h.at[i, me_f], peer) for peer in f_peers]

    def feat_finish(i, step, copies):
        for copy in copies:
            copy.wait_recv()
        width = feat_h.shape[-1]
        return sum(
            dot(feat_h[i, f], wts[step, f * width : (f + 1) * width, :]) for f in range(NL * NC)
        )

    def gather_start(step):
        own = push(gath.at[step, me_f], gath.at[step, me_f], mate)
        over = []
        for i in range(CHUNKS):
            part_of = gath.at[step, me_f, pl.ds(i * step_rows, step_rows)]
            over.append(push(part_of, part_of, across))
        return own, over

    def hand_on(step, over, i):
        over[i].wait_recv()
        came = gath.at[step, f_slots[1], pl.ds(i * step_rows, step_rows)]
        return push(came, came, mate)

    def mix(step, i):
        width = gath.shape[-1]
        at = slice(i * step_rows, (i + 1) * step_rows)
        mixed = sum(
            dot(gath[step, f, at, :], wts[step, f * width : (f + 1) * width, :])
            for f in range(NL * NC)
        ).astype(BF16)
        win[step, rows + i * step_rows : rows + (i + 1) * step_rows, :] = mixed
        src = win.at[step, pl.ds(rows + i * step_rows, step_rows)]
        to_right = remote(src, win.at[step, pl.ds(i * step_rows, step_rows)], right)
        to_left = remote(src, win.at[step, pl.ds(2 * rows + i * step_rows, step_rows)], left)

        @pl.when(has_right)
        def _():
            to_right.start()

        @pl.when(has_left)
        def _():
            to_left.start()

        return to_right, to_left

    def halo_finish(pairs):
        @pl.when(has_left)
        def _():
            for to_right, _unused in pairs:
                to_right.wait_recv()

        @pl.when(has_right)
        def _():
            for _unused, to_left in pairs:
                to_left.wait_recv()

    def halo_sent(pairs):
        @pl.when(has_right)
        def _():
            for to_right, _unused in pairs:
                to_right.wait_send()

        @pl.when(has_left)
        def _():
            for _unused, to_left in pairs:
                to_left.wait_send()

    def head_spread(step, value):
        head[step, z, yh] = value.astype(BF16)
        src = head.at[step, z, yh]
        along_y = [push(src, src, peer) for peer in y_peers]
        along_z = [push(src, src, peer) for peer in z_peers]
        return along_y, along_z

    def head_hand_on(step, along_y, along_z):
        for k in range(1, NY):
            along_y[k - 1].wait_recv()
            src = head.at[step, z, (yh + NY - k) % NY]
            along_z = along_z + [push(src, src, peer) for peer in z_peers]
        return along_z

    def head_finish(step, along_z):
        for copy in along_z:
            copy.wait_recv()
        return head[step].reshape(-1, head.shape[-1])

    heads_x = [push(h4.at[x], h4.at[x], peer) for peer in x_peers]
    own0, over0 = gather_start(0)
    z0 = z_start(0)

    load_t.wait()
    n_tiles = tiles.shape[0]
    for s in range(n_tiles):
        cell[s] = place[s, 0] * (3 * tile_rows) + (place[s, 2] + 1) * tile_rows + place[s, 1]

    def build(first, last):
        def one(i, carry):
            total = jnp.zeros((TILE, TILE), BF16)
            for s in range(n_tiles):
                total = total + jnp.where(cell[s] == i, tiles[s], jnp.zeros((TILE, TILE), BF16))
            r, w = i // (3 * tile_rows), i % (3 * tile_rows)
            dense[
                pl.ds(pl.multiple_of(r * TILE, TILE), TILE),
                pl.ds(pl.multiple_of(w * TILE, TILE), TILE),
            ] = total
            return carry

        lax.fori_loop(first, last, one, 0)

    n_cells = tile_rows * 3 * tile_rows
    quarter = n_cells // 4
    build(0, quarter)

    @pl.when(jnp.logical_not(has_left))
    def _():
        for step in range(2):
            win[step, :rows] = jnp.zeros((rows, win.shape[-1]), BF16)

    @pl.when(jnp.logical_not(has_right))
    def _():
        for step in range(2):
            win[step, 2 * rows :] = jnp.zeros((rows, win.shape[-1]), BF16)

    for copy in heads_x:
        copy.wait_recv()
    load_w.wait()
    h_rows = jnp.concatenate([h4[k] for k in range(NX)], axis=0)
    feat_a = feat_start(0, h_rows)
    hand0 = [hand_on(0, over0, 0)]
    y0 = z_finish(0, z0)
    hand0.append(hand_on(0, over0, 1))
    along_y, along_z = head_spread(0, feat_finish(0, 0, feat_a))
    build(quarter, 2 * quarter)
    hand0.append(hand_on(0, over0, 2))
    own0.wait_recv()
    hand0[0].wait_recv()
    halo0 = [mix(0, 0)]
    build(2 * quarter, 3 * quarter)
    hand0.append(hand_on(0, over0, 3))
    hand0[1].wait_recv()
    halo0.append(mix(0, 1))
    hand0[2].wait_recv()
    halo0.append(mix(0, 2))
    along_z = head_hand_on(0, along_y, along_z)
    hand0[3].wait_recv()
    halo0.append(mix(0, 3))
    x0 = y_finish(0, y0)
    build(3 * quarter, n_cells)

    load_c.wait()
    for i in range(tile_rows):
        at = slice(i * TILE, (i + 1) * TILE)
        limit = down_rows(reach[i : i + 1, :])
        bscale[at, :] = lax.rsqrt(down_rows(deg[i : i + 1, :].astype(F32)))
        for j in range(cols.shape[1] // TILE):
            lane = lax.broadcasted_iota(jnp.int32, (TILE, TILE), 1) + j * TILE
            block = cols[at, j * TILE : (j + 1) * TILE]
            cols[at, j * TILE : (j + 1) * TILE] = jnp.where(
                lane < limit, block.astype(F32), 0.0
            ).astype(BF16)
    hscale[...] = lax.rsqrt(down_rows(hdeg[pl.ds(z, 1), :].astype(F32)))
    per_head = hscale.shape[0] // NY
    h_scale = hscale[pl.ds(pl.multiple_of(yh * per_head, per_head), per_head), :]
    h_scale = jnp.concatenate([h_scale, h_scale], axis=1)

    def own_band(step):
        acc[...] = dot(dense[:, rows : 2 * rows], win[step, rows : 2 * rows, :])

    def halo_band(step):
        acc[...] += dot(dense[:, :rows], win[step, :rows, :]) + dot(
            dense[:, 2 * rows :], win[step, 2 * rows :, :]
        )

    def state(step, along):
        whole = head_finish(step, along)
        scale = jnp.concatenate([bscale[...], bscale[...]], axis=1)
        return jnp.maximum((acc[...] + dot(cols[...], whole)) * scale, 0.0)

    own_band(0)
    halo_finish(halo0)
    halo_band(0)
    gath[1, pl.ds(me_f, 1)] = state(0, along_z).astype(BF16)[None]
    own1, over1 = gather_start(1)
    head_partial(1)
    z1 = z_start(1)

    feat_b = feat_start(1, x_finish(0, x0))
    h1 = jnp.maximum(feat_finish(1, 0, feat_b) * h_scale, 0.0)
    feat_c = feat_start(2, h1)
    hand1 = [hand_on(1, over1, 0)]
    along_y, along_z = head_spread(1, feat_finish(2, 1, feat_c))
    hand1.append(hand_on(1, over1, 1))
    own1.wait_recv()
    hand1[0].wait_recv()
    halo1 = [mix(1, 0)]
    y1 = z_finish(1, z1)
    hand1.append(hand_on(1, over1, 2))
    hand1[1].wait_recv()
    halo1.append(mix(1, 1))
    hand1.append(hand_on(1, over1, 3))
    hand1[2].wait_recv()
    halo1.append(mix(1, 2))
    along_z = head_hand_on(1, along_y, along_z)
    hand1[3].wait_recv()
    halo1.append(mix(1, 3))
    x1 = y_finish(1, y1)
    own_band(1)
    halo_finish(halo1)
    halo_band(1)
    band_out[...] = state(1, along_z)
    feat_d = feat_start(3, x_finish(1, x1))
    h2 = jnp.maximum(feat_finish(3, 1, feat_d) * h_scale, 0.0)
    per = head_out.shape[0]
    mine = jnp.zeros(head_out.shape, F32)
    for k in range(NX):
        mine = mine + jnp.where(x == k, h2[k * per : (k + 1) * per, :], 0.0)
    head_out[...] = mine

    for copy in started:
        copy.wait_send()
    halo_sent(halo0)
    halo_sent(halo1)


N_COPIES = 256


def body(
    band_feats,
    head_feats,
    mix_weights,
    tile_place,
    tile_vals,
    arrow_cols,
    arrow_reach,
    arrow_rows,
    band_degree,
    head_degree,
):
    rows, width = band_feats.shape
    heads = arrow_rows.shape[0]
    per_y = heads // (NZ * NY)
    vmem = pl.BlockSpec(memory_space=pltpu.VMEM)
    smem = pl.BlockSpec(memory_space=pltpu.SMEM)
    hbm = pl.BlockSpec(memory_space=pl.ANY)
    return pl.pallas_call(
        kernel,
        out_shape=(
            jax.ShapeDtypeStruct((rows, width), F32),
            jax.ShapeDtypeStruct(head_feats.shape, F32),
        ),
        in_specs=[smem, vmem, vmem, vmem] + [hbm] * 6,
        out_specs=(vmem, vmem),
        scratch_shapes=[
            pltpu.VMEM((rows, width), F32),
            pltpu.VMEM(head_feats.shape, F32),
            pltpu.VMEM(mix_weights.shape, BF16),
            pltpu.VMEM(tile_vals.shape, BF16),
            pltpu.VMEM(arrow_cols.shape, BF16),
            pltpu.VMEM(arrow_rows.shape, BF16),
            pltpu.VMEM((rows, 3 * rows), BF16),
            pltpu.VMEM((2, NL * NC, rows, width), BF16),
            pltpu.VMEM((2, 3 * rows, width), BF16),
            pltpu.VMEM((rows, width), F32),
            pltpu.VMEM((NZ, heads // NZ, width), F32),
            pltpu.VMEM((2, NZ, heads // NZ, width), BF16),
            pltpu.VMEM((2, NZ - 1, heads // NZ, width), BF16),
            pltpu.VMEM((2, NY, per_y, width), F32),
            pltpu.VMEM((2, NY - 1, per_y, width), F32),
            pltpu.VMEM((2, per_y, width), BF16),
            pltpu.VMEM((2, NX - 1, per_y, width), BF16),
            pltpu.VMEM((4, NL * NC, per_y, width), BF16),
            pltpu.VMEM((NX, *head_feats.shape), F32),
            pltpu.VMEM((2, NZ, NY, per_y, width), BF16),
            pltpu.VMEM((heads // NZ, TILE), F32),
            pltpu.VMEM((rows, TILE), F32),
            pltpu.SMEM((tile_vals.shape[0],), jnp.int32),
            pltpu.SemaphoreType.DMA((6,)),
            pltpu.SemaphoreType.DMA((N_COPIES,)),
            pltpu.SemaphoreType.DMA((N_COPIES,)),
        ],
        compiler_params=pltpu.CompilerParams(collective_id=0, has_side_effects=True),
    )(
        tile_place,
        band_degree.reshape(-1, TILE),
        head_degree.reshape(-1, TILE),
        arrow_reach.reshape(-1, TILE),
        band_feats,
        head_feats,
        mix_weights,
        tile_vals,
        arrow_cols,
        arrow_rows,
    )


def solution(mesh):
    split = Mesh(
        mesh.devices.reshape(NZ, NY, NX, NL, NC), (*ROWS, *FEAT)
    )
    return jax.shard_map(
        body,
        mesh=split,
        in_specs=(
            P(ROWS, FEAT),
            P(ROWS, FEAT),
            P(None, None, FEAT),
            P(ROWS, None),
            P(ROWS, None, None),
            P(ROWS, None),
            P(ROWS),
            P(None, ROWS),
            P(ROWS),
            P(),
        ),
        out_specs=(P(ROWS, FEAT), P(ROWS, FEAT)),
        check_vma=False,
    )
```

```python
import functools

import jax
import jax.numpy as jnp
from jax import lax
from jax.experimental import pallas as pl
from jax.experimental.pallas import tpu as pltpu
from jax.sharding import Mesh
from jax.sharding import PartitionSpec as P

MESH = pl.DeviceIdType.MESH
F32, BF16 = jnp.float32, jnp.bfloat16
NZ, NY, NX, NL, NC = 8, 4, 4, 2, 2
ROWS = ("z", "yh", "x")
FEAT = ("yl", "core")
TILE = 128
CHUNKS = 4


def dot(a, b):
    return jnp.dot(a, b, preferred_element_type=F32)


def down_rows(line):
    return jnp.broadcast_to(line, (TILE, line.shape[-1])).T


def kernel(
    place,
    deg,
    hdeg,
    reach,
    x_hbm,
    h_hbm,
    w_hbm,
    t_hbm,
    c_hbm,
    r_hbm,
    band_out,
    head_out,
    xin,
    wts,
    tiles,
    cols,
    rws,
    rws_p,
    dense,
    gath,
    win,
    acc,
    part,
    part_b,
    xrcv,
    zsrc,
    zrcv,
    ysrc,
    yrcv,
    feat_h,
    hf,
    h4,
    relay,
    head,
    hscale,
    bscale,
    lines,
    table,
    lsem,
    ssem,
    rsem,
):
    z, yh, x = (lax.axis_index(a) for a in ROWS)
    yl, core = (lax.axis_index(a) for a in FEAT)
    rank = (z * NY + yh) * NX + x
    me_f = yl * NC + core
    rows = xin.shape[0]
    step_rows = rows // CHUNKS
    tile_rows = rows // TILE
    has_left, has_right = rank > 0, rank < NZ * NY * NX - 1

    def at_rank(r):
        return {"z": r // (NY * NX), "yh": (r // NX) % NY, "x": r % NX}

    left = at_rank(jnp.maximum(rank - 1, 0))
    right = at_rank(jnp.minimum(rank + 1, NZ * NY * NX - 1))
    z_order, y_order, x_order = [4, 3, 5, 2, 6, 1, 7], [2, 1, 3], [2, 1, 3]
    z_peers = {k: {"z": (z + k) % NZ} for k in z_order}
    y_peers = {k: {"yh": (yh + k) % NY} for k in y_order}
    x_peers = {k: {"x": (x + k) % NX} for k in x_order}
    last_x = NX - 1
    below, above = rank >= NX, rank < NZ * NY * NX - NX
    first_col, last_col = x == 0, x == last_x
    relay_right = jnp.logical_and(last_col, has_right)
    relay_left = jnp.logical_and(first_col, has_left)
    serve_right = jnp.logical_and(first_col, above)
    serve_left = jnp.logical_and(last_col, below)
    up = at_rank(jnp.minimum(rank + NX, NZ * NY * NX - 1))
    down = at_rank(jnp.maximum(rank - NX, 0))
    at_first, at_last = {"x": 0 * x}, {"x": 0 * x + last_x}
    corner = jnp.logical_or(first_col, last_col)
    greet_up, greet_down = jnp.logical_and(corner, above), jnp.logical_and(corner, below)
    mate = {"core": 1 - core}
    across = {"yl": 1 - yl}
    f_peers = [across, {"yl": 1 - yl, "core": 1 - core}, mate]
    far_slot = (1 - yl) * NC + core

    used = [0]
    started = []

    def remote(src, dst, device):
        i = used[0]
        used[0] += 1
        return pltpu.make_async_remote_copy(
            src_ref=src,
            dst_ref=dst,
            send_sem=ssem.at[i],
            recv_sem=rsem.at[i],
            device_id=device,
            device_id_type=MESH,
        )

    def push(src, dst, device):
        copy = remote(src, dst, device)
        copy.start()
        started.append(copy)
        return copy

    barrier = pltpu.get_barrier_semaphore()
    greet = [*z_peers.values(), *y_peers.values(), *x_peers.values(), *f_peers]
    for peer in greet:
        pl.semaphore_signal(barrier, inc=1, device_id=peer, device_id_type=MESH)

    @pl.when(has_left)
    def _():
        pl.semaphore_signal(barrier, inc=1, device_id=left, device_id_type=MESH)

    @pl.when(has_right)
    def _():
        pl.semaphore_signal(barrier, inc=1, device_id=right, device_id_type=MESH)

    @pl.when(greet_up)
    def _():
        pl.semaphore_signal(barrier, inc=1, device_id=up, device_id_type=MESH)

    @pl.when(greet_down)
    def _():
        pl.semaphore_signal(barrier, inc=1, device_id=down, device_id_type=MESH)

    def load(i, src, dst):
        copy = pltpu.make_async_copy(src, dst, lsem.at[i])
        copy.start()
        return copy

    load_x = load(0, x_hbm, xin)
    load_h = load(1, h_hbm, hf.at[me_f])
    load_r = load(2, r_hbm, rws)
    load_x.wait()
    load_w0 = load(3, w_hbm.at[0], wts.at[0])
    load_t = load(4, t_hbm, tiles.at[pl.ds(0, t_hbm.shape[0])])
    load_c = load(5, c_hbm, cols)
    load_w1 = load(6, w_hbm.at[1], wts.at[1])
    gath[0, pl.ds(me_f, 1)] = xin[...].astype(BF16)[None]
    load_h.wait()
    others = [has_left, has_right, greet_up, greet_down]
    pl.semaphore_wait(
        barrier, len(greet) + sum(there.astype(jnp.int32) for there in others)
    )

    def head_partial(step, weights):
        part[...] = dot(weights[...], gath[step, me_f]).reshape(part.shape)
        part_b[step] = part[...].astype(BF16)
        return [
            push(part_b.at[step, (x + k) % NX], xrcv.at[step, k - 1], x_peers[k]) for k in x_order
        ]

    def x_finish(step, copies):
        total = part[x]
        for copy in copies:
            copy.wait_recv()
        for k in range(1, NX):
            total = total + xrcv[step, k - 1].astype(F32)
        zsrc[step] = total.reshape(NZ, -1, total.shape[-1]).astype(BF16)
        return [
            push(zsrc.at[step, (z + k) % NZ], zrcv.at[step, k - 1], z_peers[k]) for k in z_order
        ]

    def z_finish(step, copies):
        for copy in copies:
            copy.wait_recv()
        total = zsrc[step, z].astype(F32)
        for k in range(1, NZ):
            total = total + zrcv[step, k - 1].astype(F32)
        ysrc[step] = total
        return [push(ysrc.at[step], yrcv.at[step, k - 1], y_peers[k]) for k in y_order]

    def y_finish(step, copies):
        for copy in copies:
            copy.wait_recv()
        total = ysrc[step]
        for k in range(1, NY):
            total = total + yrcv[step, k - 1]
        return total

    def feat_start(i, value):
        feat_h[i, pl.ds(me_f, 1)] = value.astype(BF16)[None]
        return [push(feat_h.at[i, me_f], feat_h.at[i, me_f], peer) for peer in f_peers]

    def feat_finish(i, step, copies):
        for copy in copies:
            copy.wait_recv()
        width = feat_h.shape[-1]
        return sum(
            dot(feat_h[i, f], wts[step, f * width : (f + 1) * width, :]) for f in range(NL * NC)
        )

    def over_send(step, i):
        part_of = gath.at[step, me_f, pl.ds(i * step_rows, step_rows)]
        return push(part_of, part_of, across)

    def gather_start(step, ahead):
        over = [over_send(step, i) for i in range(ahead)]
        own = push(gath.at[step, me_f], gath.at[step, me_f], mate)
        return own, over

    def hand_on(step, over, i):
        over[i].wait_recv()
        came = gath.at[step, far_slot, pl.ds(i * step_rows, step_rows)]
        return push(came, came, mate)

    def mix(step, i):
        width = gath.shape[-1]
        at = slice(i * step_rows, (i + 1) * step_rows)
        mixed = sum(
            dot(gath[step, f, at, :], wts[step, f * width : (f + 1) * width, :])
            for f in range(NL * NC)
        ).astype(BF16)
        win[step, rows + i * step_rows : rows + (i + 1) * step_rows, :] = mixed
        src = win.at[step, pl.ds(rows + i * step_rows, step_rows)]
        to_left_part = win.at[step, pl.ds(i * step_rows, step_rows)]
        to_right_part = win.at[step, pl.ds(2 * rows + i * step_rows, step_rows)]
        to_right = remote(src, to_left_part, right)
        to_left = remote(src, to_right_part, left)
        if i % 2:

            @pl.when(has_right)
            def _():
                to_right.start()

            @pl.when(has_left)
            def _():
                to_left.start()

            return to_right, to_left, None

        spare = relay.at[step, i // 2]
        by_first, by_last = remote(src, spare, at_first), remote(src, spare, at_last)
        used[0] -= 4
        pass_right = remote(spare, to_left_part, up)
        pass_left = remote(spare, to_right_part, down)
        used[0] += 2

        @pl.when(relay_right)
        def _():
            by_first.start()

        @pl.when(jnp.logical_and(has_right, jnp.logical_not(last_col)))
        def _():
            to_right.start()

        @pl.when(relay_left)
        def _():
            by_last.start()

        @pl.when(jnp.logical_and(has_left, jnp.logical_not(first_col)))
        def _():
            to_left.start()

        return to_right, to_left, (by_first, by_last, pass_right, pass_left)

    def relay_on(copies):
        by_first, by_last, pass_right, pass_left = copies[2]

        @pl.when(serve_right)
        def _():
            by_first.wait_recv()
            pass_right.start()

        @pl.when(serve_left)
        def _():
            by_last.wait_recv()
            pass_left.start()

    def halo_finish(halos):
        @pl.when(has_left)
        def _():
            for copies in halos:
                copies[0].wait_recv()

        @pl.when(has_right)
        def _():
            for copies in halos:
                copies[1].wait_recv()

    def halo_sent(halos):
        for copies in halos:
            if copies[2] is None:

                @pl.when(has_right)
                def _():
                    copies[0].wait_send()

                @pl.when(has_left)
                def _():
                    copies[1].wait_send()

                continue
            by_first, by_last, pass_right, pass_left = copies[2]

            @pl.when(relay_right)
            def _():
                by_first.wait_send()

            @pl.when(relay_left)
            def _():
                by_last.wait_send()

            @pl.when(serve_right)
            def _():
                pass_right.wait_send()

            @pl.when(serve_left)
            def _():
                pass_left.wait_send()

            @pl.when(jnp.logical_and(has_right, jnp.logical_not(last_col)))
            def _():
                copies[0].wait_send()

            @pl.when(jnp.logical_and(has_left, jnp.logical_not(first_col)))
            def _():
                copies[1].wait_send()

    piece = head.shape[-2]

    def spread(step, src, peers):
        def to_z(piece_ref):
            return [push(piece_ref, piece_ref, z_peers[k]) for k in z_order]

        return {k: push(src, src, peer) for k, peer in peers.items()}, to_z(src)

    def spread_y(value):
        head[0, z, yh] = value.astype(BF16)
        return spread(0, head.at[0, z, yh], y_peers)

    def hand_y(along_y, along_z):
        for k in (1, 3, 2):
            along_y[k].wait_recv()
            src = head.at[0, z, (yh + NY - k) % NY]
            along_z = along_z + [push(src, src, z_peers[q]) for q in z_order]
        return along_z

    def spread_x(value):
        head[1, z, x] = value.astype(BF16)
        return spread(1, head.at[1, z, x], x_peers)

    def hand_x(along_x, along_z):
        for k in (1, 3, 2):
            along_x[k].wait_recv()
            src = head.at[1, z, (x + NX - k) % NX]
            along_z = along_z + [push(src, src, z_peers[q]) for q in z_order]
        return along_z

    def head_finish(step, along_z):
        for copy in along_z:
            copy.wait_recv()
        if step:
            return jnp.concatenate([head[1, :, k].reshape(-1, head.shape[-1]) for k in range(NX)])
        return head[0].reshape(-1, head.shape[-1])

    n_tiles = place.shape[1]
    n_cols = 3 * tile_rows

    def tables():
        tile_row, tile_col, offset = (place[i : i + 1, :] for i in range(3))
        lines[...] = jnp.full(lines.shape, -1, jnp.int32)
        lines[0:1, :n_tiles] = tile_row * n_cols + (offset + 1) * tile_rows + tile_col
        line = lines[0:1, :]
        down = down_rows(line)[:n_tiles]
        slot = lax.broadcasted_iota(jnp.int32, down.shape, 0)
        lane = lax.broadcasted_iota(jnp.int32, down.shape, 1)
        later = jnp.where(jnp.logical_and(down == line, slot > lane), slot, n_tiles)
        first = jnp.where(down == lane, slot, n_tiles)
        lines[0:1, :] = jnp.min(later, axis=0, keepdims=True)
        lines[1:2, :] = jnp.min(first, axis=0, keepdims=True)
        copy = pltpu.make_async_copy(lines, table, lsem.at[7])
        copy.start()
        tiles[n_tiles] = jnp.zeros((TILE, TILE), BF16)
        return copy

    def build():
        for s in reversed(range(n_tiles - 1)):
            tiles[s] = tiles[s] + tiles[table[0, s]]
        for c in range(tile_rows * n_cols):
            r, w = c // n_cols, c % n_cols
            dense[r * TILE : (r + 1) * TILE, w * TILE : (w + 1) * TILE] = tiles[table[1, c]]

    def edges():
        @pl.when(jnp.logical_not(has_left))
        def _():
            for step in range(2):
                win[step, :rows] = jnp.zeros((rows, win.shape[-1]), BF16)

        @pl.when(jnp.logical_not(has_right))
        def _():
            for step in range(2):
                win[step, 2 * rows :] = jnp.zeros((rows, win.shape[-1]), BF16)

    def mask_cols(i):
        at = slice(i * TILE, (i + 1) * TILE)
        limit = down_rows(reach[i : i + 1, :])
        bscale[at, :] = lax.rsqrt(down_rows(deg[i : i + 1, :].astype(F32)))
        for j in range(cols.shape[1] // TILE):
            lane = lax.broadcasted_iota(jnp.int32, (TILE, TILE), 1) + j * TILE
            block = cols[at, j * TILE : (j + 1) * TILE]
            cols[at, j * TILE : (j + 1) * TILE] = jnp.where(
                lane < limit, block.astype(F32), 0.0
            ).astype(BF16)

    def permute_rows():
        per = head_out.shape[0]
        for g in range(NX):
            shape = (part.shape[1], rws.shape[0])
            to = lax.broadcasted_iota(jnp.int32, shape, 0)
            come = lax.broadcasted_iota(jnp.int32, shape, 1)
            source = (to // per) * (NX * per) + g * per + to % per
            pick = jnp.where(come == source, 1.0, 0.0).astype(BF16)
            rws_p[g * shape[0] : (g + 1) * shape[0], :] = dot(pick, rws[...]).astype(BF16)

    def own_band(step):
        acc[...] = dot(dense[:, rows : 2 * rows], win[step, rows : 2 * rows, :])

    def halo_band(step):
        acc[...] += dot(dense[:, :rows], win[step, :rows, :]) + dot(
            dense[:, 2 * rows :], win[step, 2 * rows :, :]
        )

    def state(step, along):
        whole = head_finish(step, along)
        scale = jnp.concatenate([bscale[...], bscale[...]], axis=1)
        return jnp.maximum((acc[...] + dot(cols[...], whole)) * scale, 0.0)

    heads_f = [push(hf.at[me_f], hf.at[me_f], peer) for peer in f_peers]
    own0, over0 = gather_start(0, CHUNKS)
    load_r.wait()
    x0 = head_partial(0, rws)
    tabled = tables()
    for copy in heads_f:
        copy.wait_recv()
    load_w0.wait()
    width = hf.shape[-1]
    h4[x] = sum(
        dot(hf[f].astype(BF16), wts[0, f * width : (f + 1) * width, :]) for f in range(NL * NC)
    )
    heads_x = [push(h4.at[x], h4.at[x], x_peers[k]) for k in x_order]
    load_t.wait()
    tabled.wait()
    build()
    hand0 = [hand_on(0, over0, 0)]
    for copy in heads_x:
        copy.wait_recv()
    along_y, along_z = spread_y(jnp.concatenate([h4[k] for k in range(NX)], axis=0))
    hand0.append(hand_on(0, over0, 1))
    own0.wait_recv()
    hand0[0].wait_recv()
    halo0 = [mix(0, 0)]
    z0 = x_finish(0, x0)
    hand0.append(hand_on(0, over0, 2))
    hand0[1].wait_recv()
    halo0.append(mix(0, 1))
    hand0.append(hand_on(0, over0, 3))
    hand0[2].wait_recv()
    relay_on(halo0[0])
    halo0.append(mix(0, 2))
    hand0[3].wait_recv()
    halo0.append(mix(0, 3))
    own_band(0)
    edges()
    load_c.wait()
    for i in range(tile_rows):
        mask_cols(i)
    y0 = z_finish(0, z0)
    along_z = hand_y(along_y, along_z)
    relay_on(halo0[2])
    permute_rows()
    hscale[...] = lax.rsqrt(down_rows(hdeg[pl.ds(x, 1), :].astype(F32)))
    h_scale = hscale[pl.ds(pl.multiple_of(z * piece, piece), piece), :]
    h_scale = jnp.concatenate([h_scale, h_scale], axis=1)
    halo_finish(halo0)
    halo_band(0)
    feat_b = feat_start(0, y_finish(0, y0))
    gath[1, pl.ds(me_f, 1)] = state(0, along_z).astype(BF16)[None]
    own1, over1 = gather_start(1, 2)
    x1 = head_partial(1, rws_p)
    h1 = jnp.maximum(feat_finish(0, 0, feat_b) * h_scale, 0.0)
    feat_c = feat_start(1, h1)
    over1 += [over_send(1, 2), over_send(1, 3)]
    hand1 = [hand_on(1, over1, 0)]
    load_w1.wait()
    hand1.append(hand_on(1, over1, 1))
    own1.wait_recv()
    hand1[0].wait_recv()
    halo1 = [mix(1, 0)]
    along_x, along_z = spread_x(feat_finish(1, 1, feat_c))
    z1 = x_finish(1, x1)
    hand1.append(hand_on(1, over1, 2))
    hand1[1].wait_recv()
    halo1.append(mix(1, 1))
    hand1.append(hand_on(1, over1, 3))
    hand1[2].wait_recv()
    halo1.append(mix(1, 2))
    hand1[3].wait_recv()
    halo1.append(mix(1, 3))
    relay_on(halo1[0])
    along_z = hand_x(along_x, along_z)
    y1 = z_finish(1, z1)
    own_band(1)
    relay_on(halo1[2])
    feat_d = feat_start(2, y_finish(1, y1))
    halo_finish(halo1)
    halo_band(1)
    band_out[...] = state(1, along_z)
    sums = feat_finish(2, 1, feat_d)
    per = head_out.shape[0]
    near_z = hscale.shape[0] // (per * NX * NY)
    hscale[...] = lax.rsqrt(down_rows(hdeg[pl.ds(z // near_z, 1), :].astype(F32)))
    at = pl.multiple_of((z % near_z) * NY * NX * per + yh * NX * per, NX * per)
    near = hscale[pl.ds(at, NX * per), :]
    near = jnp.concatenate([near, near], axis=1)
    mine, own_scale = jnp.zeros(head_out.shape, F32), jnp.zeros(head_out.shape, F32)
    for k in range(NY):
        mine = mine + jnp.where(yh == k, sums[k * per : (k + 1) * per, :], 0.0)
    for k in range(NX):
        own_scale = own_scale + jnp.where(x == k, near[k * per : (k + 1) * per, :], 0.0)
    head_out[...] = jnp.maximum(mine * own_scale, 0.0)

    for copy in started:
        copy.wait_send()
    halo_sent(halo0)
    halo_sent(halo1)


N_COPIES = 240


def body(
    band_feats,
    head_feats,
    mix_weights,
    tile_place,
    tile_vals,
    arrow_cols,
    arrow_reach,
    arrow_rows,
    band_degree,
    head_degree,
):
    rows, width = band_feats.shape
    heads = arrow_rows.shape[0]
    piece = heads // (NZ * NX)
    vmem = pl.BlockSpec(memory_space=pltpu.VMEM)
    hbm = pl.BlockSpec(memory_space=pl.ANY)
    return pl.pallas_call(
        kernel,
        out_shape=(
            jax.ShapeDtypeStruct((rows, width), F32),
            jax.ShapeDtypeStruct(head_feats.shape, F32),
        ),
        in_specs=[vmem] * 4 + [hbm] * 6,
        out_specs=(vmem, vmem),
        scratch_shapes=[
            pltpu.VMEM((rows, width), F32),
            pltpu.VMEM(mix_weights.shape, BF16),
            pltpu.VMEM((tile_vals.shape[0] + 1, TILE, TILE), BF16),
            pltpu.VMEM(arrow_cols.shape, BF16),
            pltpu.VMEM(arrow_rows.shape, BF16),
            pltpu.VMEM(arrow_rows.shape, BF16),
            pltpu.VMEM((rows, 3 * rows), BF16),
            pltpu.VMEM((2, NL * NC, rows, width), BF16),
            pltpu.VMEM((2, 3 * rows, width), BF16),
            pltpu.VMEM((rows, width), F32),
            pltpu.VMEM((NX, heads // NX, width), F32),
            pltpu.VMEM((2, NX, heads // NX, width), BF16),
            pltpu.VMEM((2, NX - 1, heads // NX, width), BF16),
            pltpu.VMEM((2, NZ, piece, width), BF16),
            pltpu.VMEM((2, NZ - 1, piece, width), BF16),
            pltpu.VMEM((2, piece, width), F32),
            pltpu.VMEM((2, NY - 1, piece, width), F32),
            pltpu.VMEM((3, NL * NC, piece, width), BF16),
            pltpu.VMEM((NL * NC, *head_feats.shape), F32),
            pltpu.VMEM((NX, *head_feats.shape), F32),
            pltpu.VMEM((2, 2, rows // CHUNKS, width), BF16),
            pltpu.VMEM((2, NZ, NX, piece, width), BF16),
            pltpu.VMEM((heads // NX, TILE), F32),
            pltpu.VMEM((rows, TILE), F32),
            pltpu.VMEM((8, TILE), jnp.int32),
            pltpu.SMEM((8, TILE), jnp.int32),
            pltpu.SemaphoreType.DMA((8,)),
            pltpu.SemaphoreType.DMA((N_COPIES,)),
            pltpu.SemaphoreType.DMA((N_COPIES,)),
        ],
        compiler_params=pltpu.CompilerParams(collective_id=0, has_side_effects=True),
    )(
        tile_place.T,
        band_degree.reshape(-1, TILE),
        head_degree.reshape(-1, TILE),
        arrow_reach.reshape(-1, TILE),
        band_feats,
        head_feats,
        mix_weights,
        tile_vals,
        arrow_cols,
        arrow_rows,
    )


def solution(mesh):
    split = Mesh(
        mesh.devices.reshape(NZ, NY, NX, NL, NC), (*ROWS, *FEAT)
    )
    return jax.shard_map(
        body,
        mesh=split,
        in_specs=(
            P(ROWS, FEAT),
            P(ROWS, FEAT),
            P(None, None, FEAT),
            P(ROWS, None),
            P(ROWS, None, None),
            P(ROWS, None),
            P(ROWS),
            P(None, ROWS),
            P(ROWS),
            P(),
        ),
        out_specs=(P(ROWS, FEAT), P(ROWS, FEAT)),
        check_vma=False,
    )
```

```python
import functools

import jax
import jax.numpy as jnp
from jax import lax
from jax.experimental import pallas as pl
from jax.experimental.pallas import tpu as pltpu
from jax.sharding import Mesh
from jax.sharding import PartitionSpec as P

MESH = pl.DeviceIdType.MESH
F32, BF16 = jnp.float32, jnp.bfloat16
NZ, NY, NX, NL, NC = 8, 4, 4, 2, 2
ROWS = ("z", "yh", "x")
FEAT = ("yl", "core")
TILE = 128
CHUNKS = 8


def dot(a, b):
    return jnp.dot(a, b, preferred_element_type=F32)


def down_rows(line):
    return jnp.broadcast_to(line, (TILE, line.shape[-1])).T


def kernel(
    place_hbm,
    deg_hbm,
    hdeg_hbm,
    reach_hbm,
    x_hbm,
    h_hbm,
    w_hbm,
    t_hbm,
    c_hbm,
    r_hbm,
    band_out,
    head_out,
    place,
    deg,
    hdeg,
    reach,
    xin,
    wts,
    tiles,
    cols,
    rws,
    rws_p,
    dense,
    gath,
    win,
    acc,
    part,
    part_b,
    xrcv,
    zsrc,
    zrcv,
    ysrc,
    yrcv,
    feat_h,
    hf,
    h4,
    relay,
    head,
    hscale,
    bscale,
    lines,
    table,
    lsem,
    ssem,
    rsem,
):
    z, yh, x = (lax.axis_index(a) for a in ROWS)
    yl, core = (lax.axis_index(a) for a in FEAT)
    rank = (z * NY + yh) * NX + x
    me_f = yl * NC + core
    rows = xin.shape[0]
    step_rows = rows // CHUNKS
    tile_rows = rows // TILE
    has_left, has_right = rank > 0, rank < NZ * NY * NX - 1

    def at_rank(r):
        return {"z": r // (NY * NX), "yh": (r // NX) % NY, "x": r % NX}

    left = at_rank(jnp.maximum(rank - 1, 0))
    right = at_rank(jnp.minimum(rank + 1, NZ * NY * NX - 1))
    z_order, y_order, x_order = [4, 3, 5, 2, 6, 1, 7], [2, 1, 3], [2, 1, 3]
    z_peers = {k: {"z": (z + k) % NZ} for k in z_order}
    y_peers = {k: {"yh": (yh + k) % NY} for k in y_order}
    x_peers = {k: {"x": (x + k) % NX} for k in x_order}
    last_x = NX - 1
    below, above = rank >= NX, rank < NZ * NY * NX - NX
    first_col, last_col = x == 0, x == last_x
    relay_right = jnp.logical_and(last_col, has_right)
    relay_left = jnp.logical_and(first_col, has_left)
    serve_right = jnp.logical_and(first_col, above)
    serve_left = jnp.logical_and(last_col, below)
    up = at_rank(jnp.minimum(rank + NX, NZ * NY * NX - 1))
    down = at_rank(jnp.maximum(rank - NX, 0))
    at_first, at_last = {"x": 0 * x}, {"x": 0 * x + last_x}
    corner = jnp.logical_or(first_col, last_col)
    greet_up, greet_down = jnp.logical_and(corner, above), jnp.logical_and(corner, below)
    mate = {"core": 1 - core}
    across = {"yl": 1 - yl}
    f_peers = [across, {"yl": 1 - yl, "core": 1 - core}, mate]
    far_slot = (1 - yl) * NC + core

    used = [0]
    started = []

    def remote(src, dst, device):
        i = used[0]
        used[0] += 1
        return pltpu.make_async_remote_copy(
            src_ref=src,
            dst_ref=dst,
            send_sem=ssem.at[i],
            recv_sem=rsem.at[i],
            device_id=device,
            device_id_type=MESH,
        )

    def push(src, dst, device):
        copy = remote(src, dst, device)
        copy.start()
        started.append(copy)
        return copy

    barrier = pltpu.get_barrier_semaphore()
    greet = [*z_peers.values(), *y_peers.values(), *x_peers.values(), *f_peers]
    for peer in greet:
        pl.semaphore_signal(barrier, inc=1, device_id=peer, device_id_type=MESH)

    @pl.when(has_left)
    def _():
        pl.semaphore_signal(barrier, inc=1, device_id=left, device_id_type=MESH)

    @pl.when(has_right)
    def _():
        pl.semaphore_signal(barrier, inc=1, device_id=right, device_id_type=MESH)

    @pl.when(greet_up)
    def _():
        pl.semaphore_signal(barrier, inc=1, device_id=up, device_id_type=MESH)

    @pl.when(greet_down)
    def _():
        pl.semaphore_signal(barrier, inc=1, device_id=down, device_id_type=MESH)

    def load(i, src, dst):
        copy = pltpu.make_async_copy(src, dst, lsem.at[i])
        copy.start()
        return copy

    load_x = load(0, x_hbm, xin)
    load_h = load(1, h_hbm, hf.at[me_f])
    load_r = load(2, r_hbm, rws)
    load_x.wait()
    load_w0 = load(3, w_hbm.at[0], wts.at[0])
    load_t = load(4, t_hbm, tiles.at[pl.ds(0, t_hbm.shape[0])])
    load_c = load(5, c_hbm, cols)
    load_w1 = load(6, w_hbm.at[1], wts.at[1])
    load_small = [
        load(8, place_hbm, place),
        load(9, deg_hbm, deg),
        load(10, hdeg_hbm, hdeg),
        load(11, reach_hbm, reach),
    ]
    gath[0, pl.ds(me_f, 1)] = xin[...].astype(BF16)[None]
    load_h.wait()
    others = [has_left, has_right, greet_up, greet_down]
    pl.semaphore_wait(
        barrier, len(greet) + sum(there.astype(jnp.int32) for there in others)
    )

    def head_partial(step, weights):
        part[...] = dot(weights[...], gath[step, me_f]).reshape(part.shape)
        part_b[step] = part[...].astype(BF16)
        return [
            push(part_b.at[step, (x + k) % NX], xrcv.at[step, k - 1], x_peers[k]) for k in x_order
        ]

    def x_finish(step, copies):
        total = part[x]
        for copy in copies:
            copy.wait_recv()
        for k in range(1, NX):
            total = total + xrcv[step, k - 1].astype(F32)
        zsrc[step] = total.reshape(NZ, -1, total.shape[-1]).astype(BF16)
        return [
            push(zsrc.at[step, (z + k) % NZ], zrcv.at[step, k - 1], z_peers[k]) for k in z_order
        ]

    def z_finish(step, copies):
        for copy in copies:
            copy.wait_recv()
        total = zsrc[step, z].astype(F32)
        for k in range(1, NZ):
            total = total + zrcv[step, k - 1].astype(F32)
        ysrc[step] = total
        return [push(ysrc.at[step], yrcv.at[step, k - 1], y_peers[k]) for k in y_order]

    def y_finish(step, copies):
        for copy in copies:
            copy.wait_recv()
        total = ysrc[step]
        for k in range(1, NY):
            total = total + yrcv[step, k - 1]
        return total

    def feat_start(i, value):
        feat_h[i, pl.ds(me_f, 1)] = value.astype(BF16)[None]
        return [push(feat_h.at[i, me_f], feat_h.at[i, me_f], peer) for peer in f_peers]

    def feat_finish(i, step, copies):
        for copy in copies:
            copy.wait_recv()
        width = feat_h.shape[-1]
        return sum(
            dot(feat_h[i, f], wts[step, f * width : (f + 1) * width, :]) for f in range(NL * NC)
        )

    def over_send(step, i):
        part_of = gath.at[step, me_f, pl.ds(i * step_rows, step_rows)]
        return push(part_of, part_of, across)

    def gather_start(step, ahead):
        over = [over_send(step, i) for i in range(ahead)]
        own = push(gath.at[step, me_f], gath.at[step, me_f], mate)
        return own, over

    def hand_on(step, over, i):
        over[i].wait_recv()
        came = gath.at[step, far_slot, pl.ds(i * step_rows, step_rows)]
        return push(came, came, mate)

    def mix(step, i):
        width = gath.shape[-1]
        at = slice(i * step_rows, (i + 1) * step_rows)
        mixed = sum(
            dot(gath[step, f, at, :], wts[step, f * width : (f + 1) * width, :])
            for f in range(NL * NC)
        ).astype(BF16)
        win[step, rows + i * step_rows : rows + (i + 1) * step_rows, :] = mixed
        src = win.at[step, pl.ds(rows + i * step_rows, step_rows)]
        to_left_part = win.at[step, pl.ds(i * step_rows, step_rows)]
        to_right_part = win.at[step, pl.ds(2 * rows + i * step_rows, step_rows)]
        to_right = remote(src, to_left_part, right)
        to_left = remote(src, to_right_part, left)
        if i % 2:

            @pl.when(has_right)
            def _():
                to_right.start()

            @pl.when(has_left)
            def _():
                to_left.start()

            return to_right, to_left, None

        spare = relay.at[step, i // 2]
        by_first, by_last = remote(src, spare, at_first), remote(src, spare, at_last)
        used[0] -= 4
        pass_right = remote(spare, to_left_part, up)
        pass_left = remote(spare, to_right_part, down)
        used[0] += 2

        @pl.when(relay_right)
        def _():
            by_first.start()

        @pl.when(jnp.logical_and(has_right, jnp.logical_not(last_col)))
        def _():
            to_right.start()

        @pl.when(relay_left)
        def _():
            by_last.start()

        @pl.when(jnp.logical_and(has_left, jnp.logical_not(first_col)))
        def _():
            to_left.start()

        return to_right, to_left, (by_first, by_last, pass_right, pass_left)

    def relay_on(copies):
        by_first, by_last, pass_right, pass_left = copies[2]

        @pl.when(serve_right)
        def _():
            by_first.wait_recv()
            pass_right.start()

        @pl.when(serve_left)
        def _():
            by_last.wait_recv()
            pass_left.start()

    def halo_finish(halos):
        @pl.when(has_left)
        def _():
            for copies in halos:
                copies[0].wait_recv()

        @pl.when(has_right)
        def _():
            for copies in halos:
                copies[1].wait_recv()

    def halo_sent(halos):
        for copies in halos:
            if copies[2] is None:

                @pl.when(has_right)
                def _():
                    copies[0].wait_send()

                @pl.when(has_left)
                def _():
                    copies[1].wait_send()

                continue
            by_first, by_last, pass_right, pass_left = copies[2]

            @pl.when(relay_right)
            def _():
                by_first.wait_send()

            @pl.when(relay_left)
            def _():
                by_last.wait_send()

            @pl.when(serve_right)
            def _():
                pass_right.wait_send()

            @pl.when(serve_left)
            def _():
                pass_left.wait_send()

            @pl.when(jnp.logical_and(has_right, jnp.logical_not(last_col)))
            def _():
                copies[0].wait_send()

            @pl.when(jnp.logical_and(has_left, jnp.logical_not(first_col)))
            def _():
                copies[1].wait_send()

    piece = head.shape[-2]

    def spread(step, src, peers):
        def to_z(piece_ref):
            return [push(piece_ref, piece_ref, z_peers[k]) for k in z_order]

        return {k: push(src, src, peer) for k, peer in peers.items()}, to_z(src)

    def spread_y(value):
        head[0, z, yh] = value.astype(BF16)
        return spread(0, head.at[0, z, yh], y_peers)

    def hand_y(along_y, along_z):
        for k in (1, 3, 2):
            along_y[k].wait_recv()
            src = head.at[0, z, (yh + NY - k) % NY]
            along_z = along_z + [push(src, src, z_peers[q]) for q in z_order]
        return along_z

    def spread_x(value):
        head[1, z, x] = value.astype(BF16)
        return spread(1, head.at[1, z, x], x_peers)

    def hand_x(along_x, along_z):
        for k in (1, 3, 2):
            along_x[k].wait_recv()
            src = head.at[1, z, (x + NX - k) % NX]
            along_z = along_z + [push(src, src, z_peers[q]) for q in z_order]
        return along_z

    def head_finish(step, along_z):
        for copy in along_z:
            copy.wait_recv()
        if step:
            return jnp.concatenate([head[1, :, k].reshape(-1, head.shape[-1]) for k in range(NX)])
        return head[0].reshape(-1, head.shape[-1])

    n_tiles = place.shape[1]
    n_cols = 3 * tile_rows

    def tables():
        tile_row, tile_col, offset = (place[i : i + 1, :] for i in range(3))
        lines[...] = jnp.full(lines.shape, -1, jnp.int32)
        lines[0:1, :n_tiles] = tile_row * n_cols + (offset + 1) * tile_rows + tile_col
        line = lines[0:1, :]
        down = down_rows(line)[:n_tiles]
        slot = lax.broadcasted_iota(jnp.int32, down.shape, 0)
        lane = lax.broadcasted_iota(jnp.int32, down.shape, 1)
        later = jnp.where(jnp.logical_and(down == line, slot > lane), slot, n_tiles)
        first = jnp.where(down == lane, slot, n_tiles)
        lines[0:1, :] = jnp.min(later, axis=0, keepdims=True)
        lines[1:2, :] = jnp.min(first, axis=0, keepdims=True)
        copy = pltpu.make_async_copy(lines, table, lsem.at[7])
        copy.start()
        tiles[n_tiles] = jnp.zeros((TILE, TILE), BF16)
        return copy

    def build():
        for s in reversed(range(n_tiles - 1)):
            tiles[s] = tiles[s] + tiles[table[0, s]]
        for c in range(tile_rows * n_cols):
            r, w = c // n_cols, c % n_cols
            dense[r * TILE : (r + 1) * TILE, w * TILE : (w + 1) * TILE] = tiles[table[1, c]]

    def edges():
        @pl.when(jnp.logical_not(has_left))
        def _():
            for step in range(2):
                win[step, :rows] = jnp.zeros((rows, win.shape[-1]), BF16)

        @pl.when(jnp.logical_not(has_right))
        def _():
            for step in range(2):
                win[step, 2 * rows :] = jnp.zeros((rows, win.shape[-1]), BF16)

    def mask_cols(i):
        at = slice(i * TILE, (i + 1) * TILE)
        limit = down_rows(reach[i : i + 1, :])
        bscale[at, :] = lax.rsqrt(down_rows(deg[i : i + 1, :].astype(F32)))
        for j in range(cols.shape[1] // TILE):
            lane = lax.broadcasted_iota(jnp.int32, (TILE, TILE), 1) + j * TILE
            block = cols[at, j * TILE : (j + 1) * TILE]
            cols[at, j * TILE : (j + 1) * TILE] = jnp.where(
                lane < limit, block.astype(F32), 0.0
            ).astype(BF16)

    def permute_rows():
        per = head_out.shape[0]
        for g in range(NX):
            shape = (part.shape[1], rws.shape[0])
            to = lax.broadcasted_iota(jnp.int32, shape, 0)
            come = lax.broadcasted_iota(jnp.int32, shape, 1)
            source = (to // per) * (NX * per) + g * per + to % per
            pick = jnp.where(come == source, 1.0, 0.0).astype(BF16)
            rws_p[g * shape[0] : (g + 1) * shape[0], :] = dot(pick, rws[...]).astype(BF16)

    def own_band(step):
        acc[...] = dot(dense[:, rows : 2 * rows], win[step, rows : 2 * rows, :])

    def halo_band(step):
        acc[...] += dot(dense[:, :rows], win[step, :rows, :]) + dot(
            dense[:, 2 * rows :], win[step, 2 * rows :, :]
        )

    def state(step, along):
        whole = head_finish(step, along)
        scale = jnp.concatenate([bscale[...], bscale[...]], axis=1)
        return jnp.maximum((acc[...] + dot(cols[...], whole)) * scale, 0.0)

    heads_f = [push(hf.at[me_f], hf.at[me_f], peer) for peer in f_peers]
    own0, over0 = gather_start(0, CHUNKS)
    load_r.wait()
    x0 = head_partial(0, rws)
    for copy in load_small:
        copy.wait()
    tabled = tables()
    for copy in heads_f:
        copy.wait_recv()
    load_w0.wait()
    width = hf.shape[-1]
    h4[x] = sum(
        dot(hf[f].astype(BF16), wts[0, f * width : (f + 1) * width, :]) for f in range(NL * NC)
    )
    heads_x = [push(h4.at[x], h4.at[x], x_peers[k]) for k in x_order]
    load_t.wait()
    tabled.wait()
    build()
    hand0, halo0 = [], []

    def mix_next(step, over, hand, halo):
        if len(hand) < CHUNKS:
            hand.append(hand_on(step, over, len(hand)))
        hand[len(halo)].wait_recv()
        halo.append(mix(step, len(halo)))

    hand0.append(hand_on(0, over0, 0))
    own0.wait_recv()
    mix_next(0, over0, hand0, halo0)
    mix_next(0, over0, hand0, halo0)
    mix_next(0, over0, hand0, halo0)
    for copy in heads_x:
        copy.wait_recv()
    along_y, along_z = spread_y(jnp.concatenate([h4[k] for k in range(NX)], axis=0))
    mix_next(0, over0, hand0, halo0)
    mix_next(0, over0, hand0, halo0)
    z0 = x_finish(0, x0)
    mix_next(0, over0, hand0, halo0)
    relay_on(halo0[0])
    mix_next(0, over0, hand0, halo0)
    mix_next(0, over0, hand0, halo0)
    relay_on(halo0[2])
    edges()
    own_band(0)
    relay_on(halo0[4])
    along_z = hand_y(along_y, along_z)
    relay_on(halo0[6])
    y0 = z_finish(0, z0)
    load_c.wait()
    for i in range(tile_rows):
        mask_cols(i)
    permute_rows()
    hscale[...] = lax.rsqrt(down_rows(hdeg[pl.ds(x, 1), :].astype(F32)))
    h_scale = hscale[pl.ds(pl.multiple_of(z * piece, piece), piece), :]
    h_scale = jnp.concatenate([h_scale, h_scale], axis=1)
    halo_finish(halo0)
    halo_band(0)
    feat_b = feat_start(0, y_finish(0, y0))
    gath[1, pl.ds(me_f, 1)] = state(0, along_z).astype(BF16)[None]
    own1, over1 = gather_start(1, CHUNKS)
    x1 = head_partial(1, rws_p)
    h1 = jnp.maximum(feat_finish(0, 0, feat_b) * h_scale, 0.0)
    feat_c = feat_start(1, h1)
    load_w1.wait()
    hand1, halo1 = [hand_on(1, over1, 0)], []
    own1.wait_recv()
    for _i in range(3):
        mix_next(1, over1, hand1, halo1)
    z1 = x_finish(1, x1)
    for _i in range(3):
        mix_next(1, over1, hand1, halo1)
    relay_on(halo1[0])
    mix_next(1, over1, hand1, halo1)
    mix_next(1, over1, hand1, halo1)
    relay_on(halo1[2])
    along_x, along_z = spread_x(feat_finish(1, 1, feat_c))
    relay_on(halo1[4])
    own_band(1)
    y1 = z_finish(1, z1)
    relay_on(halo1[6])
    along_z = hand_x(along_x, along_z)
    feat_d = feat_start(2, y_finish(1, y1))
    halo_finish(halo1)
    halo_band(1)
    band_out[...] = state(1, along_z)
    sums = feat_finish(2, 1, feat_d)
    per = head_out.shape[0]
    near_z = hscale.shape[0] // (per * NX * NY)
    hscale[...] = lax.rsqrt(down_rows(hdeg[pl.ds(z // near_z, 1), :].astype(F32)))
    at = pl.multiple_of((z % near_z) * NY * NX * per + yh * NX * per, NX * per)
    near = hscale[pl.ds(at, NX * per), :]
    near = jnp.concatenate([near, near], axis=1)
    mine, own_scale = jnp.zeros(head_out.shape, F32), jnp.zeros(head_out.shape, F32)
    for k in range(NY):
        mine = mine + jnp.where(yh == k, sums[k * per : (k + 1) * per, :], 0.0)
    for k in range(NX):
        own_scale = own_scale + jnp.where(x == k, near[k * per : (k + 1) * per, :], 0.0)
    head_out[...] = jnp.maximum(mine * own_scale, 0.0)

    for copy in started:
        copy.wait_send()
    halo_sent(halo0)
    halo_sent(halo1)


def write_out(band, head, band_out, head_out, sem):
    copies = [
        pltpu.make_async_copy(src, dst, sem.at[i])
        for i, (src, dst) in enumerate(((band, band_out), (head, head_out)))
    ]
    for copy in copies:
        copy.start()
    for copy in copies:
        copy.wait()


N_COPIES = 240


def body(
    band_feats,
    head_feats,
    mix_weights,
    tile_place,
    tile_vals,
    arrow_cols,
    arrow_reach,
    arrow_rows,
    band_degree,
    head_degree,
):
    rows, width = band_feats.shape
    heads = arrow_rows.shape[0]
    piece = heads // (NZ * NX)
    vmem = pl.BlockSpec(memory_space=pltpu.VMEM)
    hbm = pl.BlockSpec(memory_space=pl.ANY)
    results = pl.pallas_call(
        kernel,
        out_shape=(pltpu.VMEM((rows, width), F32), pltpu.VMEM(head_feats.shape, F32)),
        in_specs=[hbm] * 10,
        out_specs=(vmem, vmem),
        scratch_shapes=[
            pltpu.VMEM(tile_place.shape[::-1], jnp.int32),
            pltpu.VMEM((rows // TILE, TILE), jnp.int32),
            pltpu.VMEM((heads // TILE, TILE), jnp.int32),
            pltpu.VMEM((rows // TILE, TILE), jnp.int32),
            pltpu.VMEM((rows, width), F32),
            pltpu.VMEM(mix_weights.shape, BF16),
            pltpu.VMEM((tile_vals.shape[0] + 1, TILE, TILE), BF16),
            pltpu.VMEM(arrow_cols.shape, BF16),
            pltpu.VMEM(arrow_rows.shape, BF16),
            pltpu.VMEM(arrow_rows.shape, BF16),
            pltpu.VMEM((rows, 3 * rows), BF16),
            pltpu.VMEM((2, NL * NC, rows, width), BF16),
            pltpu.VMEM((2, 3 * rows, width), BF16),
            pltpu.VMEM((rows, width), F32),
            pltpu.VMEM((NX, heads // NX, width), F32),
            pltpu.VMEM((2, NX, heads // NX, width), BF16),
            pltpu.VMEM((2, NX - 1, heads // NX, width), BF16),
            pltpu.VMEM((2, NZ, piece, width), BF16),
            pltpu.VMEM((2, NZ - 1, piece, width), BF16),
            pltpu.VMEM((2, piece, width), F32),
            pltpu.VMEM((2, NY - 1, piece, width), F32),
            pltpu.VMEM((3, NL * NC, piece, width), BF16),
            pltpu.VMEM((NL * NC, *head_feats.shape), F32),
            pltpu.VMEM((NX, *head_feats.shape), F32),
            pltpu.VMEM((2, CHUNKS // 2, rows // CHUNKS, width), BF16),
            pltpu.VMEM((2, NZ, NX, piece, width), BF16),
            pltpu.VMEM((heads // NX, TILE), F32),
            pltpu.VMEM((rows, TILE), F32),
            pltpu.VMEM((8, TILE), jnp.int32),
            pltpu.SMEM((8, TILE), jnp.int32),
            pltpu.SemaphoreType.DMA((12,)),
            pltpu.SemaphoreType.DMA((N_COPIES,)),
            pltpu.SemaphoreType.DMA((N_COPIES,)),
        ],
        compiler_params=pltpu.CompilerParams(collective_id=0, has_side_effects=True),
    )(
        tile_place.T,
        band_degree.reshape(-1, TILE),
        head_degree.reshape(-1, TILE),
        arrow_reach.reshape(-1, TILE),
        band_feats,
        head_feats,
        mix_weights,
        tile_vals,
        arrow_cols,
        arrow_rows,
    )
    return pl.pallas_call(
        write_out,
        out_shape=(
            jax.ShapeDtypeStruct((rows, width), F32),
            jax.ShapeDtypeStruct(head_feats.shape, F32),
        ),
        in_specs=[vmem, vmem],
        out_specs=(hbm, hbm),
        scratch_shapes=[pltpu.SemaphoreType.DMA((2,))],
    )(*(pltpu.with_memory_space_constraint(r, pltpu.VMEM) for r in results))


def solution(mesh):
    split = Mesh(
        mesh.devices.reshape(NZ, NY, NX, NL, NC), (*ROWS, *FEAT)
    )
    return jax.shard_map(
        body,
        mesh=split,
        in_specs=(
            P(ROWS, FEAT),
            P(ROWS, FEAT),
            P(None, None, FEAT),
            P(ROWS, None),
            P(ROWS, None, None),
            P(ROWS, None),
            P(ROWS),
            P(None, ROWS),
            P(ROWS),
            P(),
        ),
        out_specs=(P(ROWS, FEAT), P(ROWS, FEAT)),
        check_vma=False,
    )
```

```python
import functools

import jax
import jax.numpy as jnp
from jax import lax
from jax.experimental import pallas as pl
from jax.experimental.pallas import tpu as pltpu
from jax.sharding import Mesh
from jax.sharding import PartitionSpec as P

MESH = pl.DeviceIdType.MESH
F32, BF16 = jnp.float32, jnp.bfloat16
NZ, NY, NX, NL, NC = 8, 4, 4, 2, 2
ROWS = ("z", "yh", "x")
FEAT = ("yl", "core")
TILE = 128
CHUNKS = 8
RELAYED = (0, 1, 2, 4)
VIA = (6, 7)


def dot(a, b):
    return jnp.dot(a, b, preferred_element_type=F32)


def down_rows(line):
    return jnp.broadcast_to(line, (TILE, line.shape[-1])).T


def kernel(
    place_hbm,
    deg_hbm,
    hdeg_hbm,
    reach_hbm,
    x_hbm,
    h_hbm,
    w_hbm,
    t_hbm,
    c_hbm,
    r_hbm,
    band_out,
    head_out,
    place,
    deg,
    hdeg,
    reach,
    xin,
    wts,
    tiles,
    cols,
    rws,
    rws_p,
    dense,
    gath,
    win,
    acc,
    part,
    part_b,
    xrcv,
    zsrc,
    zrcv,
    ysrc,
    yrcv,
    yout,
    yown,
    hf_last,
    feat_h,
    hf,
    h4,
    relay,
    through,
    head,
    half4,
    half_b,
    cols_p,
    hscale,
    bscale,
    lines,
    table,
    lsem,
    ssem,
    rsem,
):
    z, yh, x = (lax.axis_index(a) for a in ROWS)
    yl, core = (lax.axis_index(a) for a in FEAT)
    rank = (z * NY + yh) * NX + x
    me_f = yl * NC + core
    rows = xin.shape[0]
    step_rows = rows // CHUNKS
    tile_rows = rows // TILE
    has_left, has_right = rank > 0, rank < NZ * NY * NX - 1

    def at_rank(r):
        return {"z": r // (NY * NX), "yh": (r // NX) % NY, "x": r % NX}

    left = at_rank(jnp.maximum(rank - 1, 0))
    right = at_rank(jnp.minimum(rank + 1, NZ * NY * NX - 1))
    z_order, y_order, x_order = [4, 3, 5, 2, 6, 1, 7], [2, 1, 3], [2, 1, 3]
    z_peers = {k: {"z": (z + k) % NZ} for k in z_order}
    y_peers = {k: {"yh": (yh + k) % NY} for k in y_order}
    x_peers = {k: {"x": (x + k) % NX} for k in x_order}
    last_x = NX - 1
    below, above = rank >= NX, rank < NZ * NY * NX - NX
    first_col, last_col = x == 0, x == last_x
    relay_right = jnp.logical_and(last_col, has_right)
    relay_left = jnp.logical_and(first_col, has_left)
    serve_right = jnp.logical_and(first_col, above)
    serve_left = jnp.logical_and(last_col, below)
    up = at_rank(jnp.minimum(rank + NX, NZ * NY * NX - 1))
    down = at_rank(jnp.maximum(rank - NX, 0))
    at_first, at_last = {"x": 0 * x}, {"x": 0 * x + last_x}
    corner = jnp.logical_or(first_col, last_col)
    inner = jnp.logical_not(corner)
    beside = {"x": x + 1 - 2 * (x % 2)}
    beyond = {"x": x + 1 - 2 * (x % 2), "yl": 1 - yl}
    greet_up, greet_down = jnp.logical_and(corner, above), jnp.logical_and(corner, below)
    mate = {"core": 1 - core}
    across = {"yl": 1 - yl}
    f_peers = [across, {"yl": 1 - yl, "core": 1 - core}, mate]
    far_slot = (1 - yl) * NC + core

    n_send, n_recv, ends = [0], [0], []

    def fresh(count):
        count[0] += 1
        return count[0] - 1

    def copy_of(src, dst, device, s, r):
        return pltpu.make_async_remote_copy(
            src_ref=src,
            dst_ref=dst,
            send_sem=ssem.at[s],
            recv_sem=rsem.at[r],
            device_id=device,
            device_id_type=MESH,
        )

    def whole_of(like, s, r):
        return copy_of(like, like, mate, s, r)

    def group(like, copies):
        s, r = fresh(n_send), fresh(n_recv)
        for src, dst, device in copies:
            copy_of(src, dst, device, s, r).start()
        whole = whole_of(like, s, r)
        ends.append(whole)
        return [whole]

    def push(src, dst, device, s):
        copy = copy_of(src, dst, device, s, fresh(n_recv))
        copy.start()
        return copy

    shared = {}

    def shared_send(name, step, like):
        if (name, step) not in shared:
            shared[name, step] = fresh(n_send)
            ends.append(whole_of(like, shared[name, step], 0))
        return shared[name, step]

    barrier = pltpu.get_barrier_semaphore()
    greet = [*z_peers.values(), *y_peers.values(), *x_peers.values(), *f_peers, beyond]
    for peer in greet:
        pl.semaphore_signal(barrier, inc=1, device_id=peer, device_id_type=MESH)

    @pl.when(has_left)
    def _():
        pl.semaphore_signal(barrier, inc=1, device_id=left, device_id_type=MESH)

    @pl.when(has_right)
    def _():
        pl.semaphore_signal(barrier, inc=1, device_id=right, device_id_type=MESH)

    @pl.when(greet_up)
    def _():
        pl.semaphore_signal(barrier, inc=1, device_id=up, device_id_type=MESH)

    @pl.when(greet_down)
    def _():
        pl.semaphore_signal(barrier, inc=1, device_id=down, device_id_type=MESH)

    def load(i, src, dst):
        copy = pltpu.make_async_copy(src, dst, lsem.at[i])
        copy.start()
        return copy

    load_x = load(0, x_hbm, xin)
    load_h = load(1, h_hbm, hf.at[me_f])
    load_r = load(2, r_hbm, rws)
    load_x.wait()
    load_w0 = load(3, w_hbm.at[0], wts.at[0])
    load_t = load(4, t_hbm, tiles.at[pl.ds(0, t_hbm.shape[0])])
    load_c = load(5, c_hbm, cols)
    load_w1 = load(6, w_hbm.at[1], wts.at[1])
    load_small = [
        load(8, place_hbm, place),
        load(9, deg_hbm, deg),
        load(10, hdeg_hbm, hdeg),
        load(11, reach_hbm, reach),
    ]
    gath[0, pl.ds(me_f, 1)] = xin[...].astype(BF16)[None]
    load_h.wait()
    others = [has_left, has_right, greet_up, greet_down]
    pl.semaphore_wait(
        barrier, len(greet) + sum(there.astype(jnp.int32) for there in others)
    )

    def head_partial(step, weights):
        part[...] = dot(weights[...], gath[step, me_f]).reshape(part.shape)
        part_b[step] = part[...].astype(BF16)
        return group(
            xrcv.at[step],
            [(part_b.at[step, (x + k) % NX], xrcv.at[step, k - 1], x_peers[k]) for k in x_order],
        )

    def x_finish(step, copies):
        total = part[x]
        for copy in copies:
            copy.wait_recv()
        for k in range(1, NX):
            total = total + xrcv[step, k - 1].astype(F32)
        zsrc[step] = total.reshape(NZ, -1, total.shape[-1]).astype(BF16)
        return group(
            zrcv.at[step],
            [(zsrc.at[step, (z + k) % NZ], zrcv.at[step, k - 1], z_peers[k]) for k in z_order],
        )

    def z_finish(step, copies):
        for copy in copies:
            copy.wait_recv()
        total = zsrc[step, z].astype(F32)
        for k in range(1, NZ):
            total = total + zrcv[step, k - 1].astype(F32)
        if step:
            per = head_out.shape[0]
            for k in range(NY):
                yout[k] = total[k * per : (k + 1) * per]
            return group(
                yown, [(yout.at[(yh + k) % NY], yown.at[k - 1], y_peers[k]) for k in y_order]
            )
        ysrc[...] = total.astype(BF16)
        return group(yrcv, [(ysrc, yrcv.at[k - 1], y_peers[k]) for k in y_order])

    def y_finish(step, copies):
        for copy in copies:
            copy.wait_recv()
        if step:
            return yout[yh] + sum(yown[k] for k in range(NY - 1))
        return ysrc[...].astype(F32) + sum(yrcv[k].astype(F32) for k in range(NY - 1))

    def last_start(value):
        hf_last[me_f] = value
        return spread_f(hf_last)

    def spread_f(ref):
        return group(
            ref.at[pl.ds(0, len(f_peers))], [(ref.at[me_f], ref.at[me_f], peer) for peer in f_peers]
        )

    def last_finish(copies):
        for copy in copies:
            copy.wait_recv()
        width = hf_last.shape[-1]
        return sum(
            dot(hf_last[f].astype(BF16), wts[1, f * width : (f + 1) * width, :])
            for f in range(NL * NC)
        )

    def feat_start(i, value):
        feat_h[i, pl.ds(me_f, 1)] = value.astype(BF16)[None]
        return spread_f(feat_h.at[i])

    def feat_finish(i, step, copies):
        for copy in copies:
            copy.wait_recv()
        width = feat_h.shape[-1]
        return sum(
            dot(feat_h[i, f], wts[step, f * width : (f + 1) * width, :]) for f in range(NL * NC)
        )

    vias = []
    via_s, via_r = fresh(n_send), fresh(n_recv)
    all_vias = whole_of(through, via_s, via_r)

    def over_send(step, i):
        part_of = gath.at[step, me_f, pl.ds(i * step_rows, step_rows)]
        s = shared_send("over", step, gath.at[step, 0])
        if step or i not in VIA:
            return push(part_of, part_of, across, s)
        spare = through.at[VIA.index(i)]
        r = fresh(n_recv)
        straight = copy_of(part_of, part_of, across, s, r)
        beside_copy = copy_of(part_of, spare, beside, s, via_r)
        vias.append(copy_of(spare, part_of, beyond, via_s, r))

        @pl.when(corner)
        def _():
            beside_copy.start()

        @pl.when(inner)
        def _():
            straight.start()

        return straight

    def cross_on():
        @pl.when(inner)
        def _():
            all_vias.wait_recv()
            for onward in vias:
                onward.start()

    def via_sent():
        @pl.when(inner)
        def _():
            all_vias.wait_send()

    def gather_start(step, ahead):
        over = [over_send(step, i) for i in range(ahead)]
        mine = gath.at[step, me_f]
        return group(mine, [(mine, mine, mate)])[0], over

    def hand_on(step, over, i):
        over[i].wait_recv()
        came = gath.at[step, far_slot, pl.ds(i * step_rows, step_rows)]
        return push(came, came, mate, shared_send("hand", step, gath.at[step, 0]))

    halo_sems = [[fresh(n_send) for _i in range(3)] + [fresh(n_recv) for _i in range(2)] for _j in range(2)]

    def mix(step, i):
        width = gath.shape[-1]
        at = slice(i * step_rows, (i + 1) * step_rows)
        mixed = sum(
            dot(gath[step, f, at, :], wts[step, f * width : (f + 1) * width, :])
            for f in range(NL * NC)
        ).astype(BF16)
        win[step, rows + i * step_rows : rows + (i + 1) * step_rows, :] = mixed
        src = win.at[step, pl.ds(rows + i * step_rows, step_rows)]
        to_left_part = win.at[step, pl.ds(i * step_rows, step_rows)]
        to_right_part = win.at[step, pl.ds(2 * rows + i * step_rows, step_rows)]
        s_right, s_left, s_pass, r_right, r_left = halo_sems[step]
        to_right = copy_of(src, to_left_part, right, s_right, r_right)
        to_left = copy_of(src, to_right_part, left, s_left, r_left)
        if i not in RELAYED:

            @pl.when(has_right)
            def _():
                to_right.start()

            @pl.when(has_left)
            def _():
                to_left.start()

            return to_right, to_left, None

        spare = relay.at[step, RELAYED.index(i)]
        r_spare = fresh(n_recv)
        by_first = copy_of(src, spare, at_first, s_right, r_spare)
        by_last = copy_of(src, spare, at_last, s_left, r_spare)
        pass_right = copy_of(spare, to_left_part, up, s_pass, r_right)
        pass_left = copy_of(spare, to_right_part, down, s_pass, r_left)

        @pl.when(relay_right)
        def _():
            by_first.start()

        @pl.when(jnp.logical_and(has_right, jnp.logical_not(last_col)))
        def _():
            to_right.start()

        @pl.when(relay_left)
        def _():
            by_last.start()

        @pl.when(jnp.logical_and(has_left, jnp.logical_not(first_col)))
        def _():
            to_left.start()

        return to_right, to_left, (by_first, by_last, pass_right, pass_left)

    def relay_on(copies):
        by_first, by_last, pass_right, pass_left = copies[2]

        @pl.when(serve_right)
        def _():
            by_first.wait_recv()
            pass_right.start()

        @pl.when(serve_left)
        def _():
            by_last.wait_recv()
            pass_left.start()

    def halo_whole(step):
        s_right, s_left, s_pass, r_right, r_left = halo_sems[step]
        block = win.at[step, pl.ds(0, rows)]
        return (
            whole_of(block, s_right, r_right),
            whole_of(block, s_left, r_left),
            whole_of(relay.at[step], s_pass, r_left),
        )

    def halo_finish(step):
        rightward, leftward, _unused = halo_whole(step)

        @pl.when(has_left)
        def _():
            rightward.wait_recv()

        @pl.when(has_right)
        def _():
            leftward.wait_recv()

    def halo_sent(step):
        rightward, leftward, passed = halo_whole(step)

        @pl.when(has_right)
        def _():
            rightward.wait_send()

        @pl.when(has_left)
        def _():
            leftward.wait_send()

        @pl.when(jnp.logical_or(serve_right, serve_left))
        def _():
            passed.wait_send()

    piece = head.shape[-2]
    half = head.shape[-1]

    z_sems = [(fresh(n_send), fresh(n_recv)) for _i in range(2)]

    def all_z(step):
        return whole_of(head.at[step, pl.ds(0, NZ - 1)], *z_sems[step])

    def hand_z(step, src):
        for k in z_order:
            copy_of(src, src, z_peers[k], *z_sems[step]).start()

    def spread(step, src, peers):
        s = shared_send("head", step, head.at[step, 0, pl.ds(0, len(peers))])
        along = {k: push(src, src, peer, s) for k, peer in peers.items()}
        hand_z(step, src)
        return along

    def spread_y(value):
        head[0, z, yh] = value.astype(BF16)
        return spread(0, head.at[0, z, yh], y_peers)

    def hand_y(along_y):
        for k in (1, 3, 2):
            along_y[k].wait_recv()
            hand_z(0, head.at[0, z, (yh + NY - k) % NY])

    def second_y(copies):
        for copy in copies:
            copy.wait_recv()
        lines = jnp.concatenate([half4[i] for i in range(NZ)], axis=0)
        per = lines.shape[0]
        at = pl.ds(pl.multiple_of(yh * per, per), per)
        half_b[0, x, at] = lines.astype(BF16)
        src = half_b.at[0, x, at]
        return group(
            half_b.at[0, 0, pl.ds(0, (NY - 1) * per)], [(src, src, y_peers[k]) for k in y_order]
        )

    def second_x(step, copies):
        for copy in copies:
            copy.wait_recv()
        src = half_b.at[step, x]
        return group(half_b.at[step, pl.ds(0, NX - 1)], [(src, src, x_peers[k]) for k in x_order])

    def spread_x(value):
        head[1, z, x] = value[:, :half].astype(BF16)
        at = pl.ds(pl.multiple_of(z * piece, piece), piece)
        half_b[1, x, at] = value[:, half:].astype(BF16)
        src = half_b.at[1, x, at]
        second = group(
            half_b.at[1, 0, pl.ds(0, (NZ - 1) * piece)], [(src, src, z_peers[k]) for k in z_order]
        )
        return spread(1, head.at[1, z, x], x_peers), second

    def hand_x(along_x):
        for k in (1, 3, 2):
            along_x[k].wait_recv()
            hand_z(1, head.at[1, z, (x + NX - k) % NX])

    def head_band(step, along_x):
        all_z(step).wait_recv()
        if step:
            first = jnp.concatenate([head[1, :, k].reshape(-1, half) for k in range(NX)])
        else:
            first = head[0].reshape(-1, half)
        one = dot(cols[...], first)
        for copy in along_x:
            copy.wait_recv()
        by = cols if step else cols_p
        two = dot(by[...], half_b[step].reshape(-1, half))
        return jnp.concatenate([one, two], axis=1)

    def permute_cols():
        per = head_out.shape[0]
        for g in range(NX):
            shape = (cols.shape[1], part.shape[1])
            come = lax.broadcasted_iota(jnp.int32, shape, 0)
            to = lax.broadcasted_iota(jnp.int32, shape, 1)
            row = (to // per) % NZ * (NY * NX * per) + to // (NZ * per) * (NX * per)
            pick = jnp.where(come == row + g * per + to % per, 1.0, 0.0).astype(BF16)
            cols_p[:, g * shape[1] : (g + 1) * shape[1]] = dot(cols[...], pick).astype(BF16)

    n_tiles = place.shape[1]
    n_cols = 3 * tile_rows

    def tables():
        tile_row, tile_col, offset = (place[i : i + 1, :] for i in range(3))
        lines[...] = jnp.full(lines.shape, -1, jnp.int32)
        lines[0:1, :n_tiles] = tile_row * n_cols + (offset + 1) * tile_rows + tile_col
        line = lines[0:1, :]
        down = down_rows(line)[:n_tiles]
        slot = lax.broadcasted_iota(jnp.int32, down.shape, 0)
        lane = lax.broadcasted_iota(jnp.int32, down.shape, 1)
        later = jnp.where(jnp.logical_and(down == line, slot > lane), slot, n_tiles)
        first = jnp.where(down == lane, slot, n_tiles)
        lines[0:1, :] = jnp.min(later, axis=0, keepdims=True)
        lines[1:2, :] = jnp.min(first, axis=0, keepdims=True)
        copy = pltpu.make_async_copy(lines, table, lsem.at[7])
        copy.start()
        tiles[n_tiles] = jnp.zeros((TILE, TILE), BF16)
        return copy

    def build():
        for s in reversed(range(n_tiles - 1)):
            tiles[s] = tiles[s] + tiles[table[0, s]]
        for c in range(tile_rows * n_cols):
            r, w = c // n_cols, c % n_cols
            dense[r * TILE : (r + 1) * TILE, w * TILE : (w + 1) * TILE] = tiles[table[1, c]]

    def edges():
        @pl.when(jnp.logical_not(has_left))
        def _():
            for step in range(2):
                win[step, :rows] = jnp.zeros((rows, win.shape[-1]), BF16)

        @pl.when(jnp.logical_not(has_right))
        def _():
            for step in range(2):
                win[step, 2 * rows :] = jnp.zeros((rows, win.shape[-1]), BF16)

    def mask_cols(i):
        at = slice(i * TILE, (i + 1) * TILE)
        limit = down_rows(reach[i : i + 1, :])
        bscale[at, :] = lax.rsqrt(down_rows(deg[i : i + 1, :].astype(F32)))
        for j in range(cols.shape[1] // TILE):
            lane = lax.broadcasted_iota(jnp.int32, (TILE, TILE), 1) + j * TILE
            block = cols[at, j * TILE : (j + 1) * TILE]
            cols[at, j * TILE : (j + 1) * TILE] = jnp.where(
                lane < limit, block.astype(F32), 0.0
            ).astype(BF16)

    def permute_rows():
        per = head_out.shape[0]
        for g in range(NX):
            shape = (part.shape[1], rws.shape[0])
            to = lax.broadcasted_iota(jnp.int32, shape, 0)
            come = lax.broadcasted_iota(jnp.int32, shape, 1)
            source = (to // per) * (NX * per) + g * per + to % per
            pick = jnp.where(come == source, 1.0, 0.0).astype(BF16)
            rws_p[g * shape[0] : (g + 1) * shape[0], :] = dot(pick, rws[...]).astype(BF16)

    def own_band(step):
        acc[...] = dot(dense[:, rows : 2 * rows], win[step, rows : 2 * rows, :])

    def halo_band(step):
        acc[...] += dot(dense[:, :rows], win[step, :rows, :]) + dot(
            dense[:, 2 * rows :], win[step, 2 * rows :, :]
        )

    def state(step, along_x):
        from_head = head_band(step, along_x)
        scale = jnp.concatenate([bscale[...], bscale[...]], axis=1)
        return jnp.maximum((acc[...] + from_head) * scale, 0.0)

    heads_f = spread_f(hf)
    own0, over0 = gather_start(0, CHUNKS)
    load_r.wait()
    x0 = head_partial(0, rws)
    for copy in load_small:
        copy.wait()
    tabled = tables()
    for copy in heads_f:
        copy.wait_recv()
    load_w0.wait()
    width = hf.shape[-1]
    own_rows = sum(
        dot(hf[f].astype(BF16), wts[0, f * width : (f + 1) * width, :]) for f in range(NL * NC)
    )
    h4[x] = own_rows[:, :half]
    half4[z] = own_rows[:, half:]
    heads_x = group(h4.at[pl.ds(0, NX - 1)], [(h4.at[x], h4.at[x], x_peers[k]) for k in x_order])
    second = group(
        half4.at[pl.ds(0, NZ - 1)], [(half4.at[z], half4.at[z], z_peers[k]) for k in z_order]
    )
    hand0, halo0 = [], []

    def mix_next(step, over, hand, halo):
        if len(hand) < CHUNKS:
            hand.append(hand_on(step, over, len(hand)))
        hand[len(halo)].wait_recv()
        halo.append(mix(step, len(halo)))

    cross_on()
    hand0.append(hand_on(0, over0, 0))
    own0.wait_recv()
    mix_next(0, over0, hand0, halo0)
    mix_next(0, over0, hand0, halo0)
    mix_next(0, over0, hand0, halo0)
    for copy in heads_x:
        copy.wait_recv()
    along_y = spread_y(jnp.concatenate([h4[k] for k in range(NX)], axis=0))
    mix_next(0, over0, hand0, halo0)
    mix_next(0, over0, hand0, halo0)
    z0 = x_finish(0, x0)
    relay_on(halo0[0])
    mix_next(0, over0, hand0, halo0)
    relay_on(halo0[1])
    second = second_y(second)
    mix_next(0, over0, hand0, halo0)
    relay_on(halo0[2])
    mix_next(0, over0, hand0, halo0)
    load_t.wait()
    tabled.wait()
    build()
    relay_on(halo0[4])
    hand_y(along_y)
    edges()
    own_band(0)
    second = second_x(0, second)
    y0 = z_finish(0, z0)
    load_c.wait()
    for i in range(tile_rows):
        mask_cols(i)
    permute_cols()
    permute_rows()
    hscale[...] = lax.rsqrt(down_rows(hdeg[pl.ds(x, 1), :].astype(F32)))
    h_scale = hscale[pl.ds(pl.multiple_of(z * piece, piece), piece), :]
    h_scale = jnp.concatenate([h_scale, h_scale], axis=1)
    halo_finish(0)
    halo_band(0)
    gath[1, pl.ds(me_f, 1)] = state(0, second).astype(BF16)[None]
    feat_b = feat_start(0, y_finish(0, y0))
    own1, over1 = gather_start(1, CHUNKS)
    x1 = head_partial(1, rws_p)
    load_w1.wait()
    hand1, halo1 = [hand_on(1, over1, 0)], []
    own1.wait_recv()
    for _i in range(2):
        mix_next(1, over1, hand1, halo1)
    h1 = jnp.maximum(feat_finish(0, 0, feat_b) * h_scale, 0.0)
    feat_c = feat_start(1, h1)
    for _i in range(2):
        mix_next(1, over1, hand1, halo1)
    z1 = x_finish(1, x1)
    mix_next(1, over1, hand1, halo1)
    relay_on(halo1[0])
    mix_next(1, over1, hand1, halo1)
    relay_on(halo1[1])
    mix_next(1, over1, hand1, halo1)
    relay_on(halo1[2])
    mix_next(1, over1, hand1, halo1)
    along_x, second = spread_x(feat_finish(1, 1, feat_c))
    relay_on(halo1[4])
    y1 = z_finish(1, z1)
    hand_x(along_x)
    own_band(1)
    second = second_x(1, second)
    feat_d = last_start(y_finish(1, y1))
    halo_finish(1)
    halo_band(1)
    band_out[...] = state(1, second)
    sums = last_finish(feat_d)
    per = head_out.shape[0]
    near_z = hscale.shape[0] // (per * NX * NY)
    hscale[...] = lax.rsqrt(down_rows(hdeg[pl.ds(z // near_z, 1), :].astype(F32)))
    at = pl.multiple_of((z % near_z) * NY * NX * per + yh * NX * per, NX * per)
    near = hscale[pl.ds(at, NX * per), :]
    near = jnp.concatenate([near, near], axis=1)
    own_scale = jnp.zeros(head_out.shape, F32)
    for k in range(NX):
        own_scale = own_scale + jnp.where(x == k, near[k * per : (k + 1) * per, :], 0.0)
    head_out[...] = jnp.maximum(sums * own_scale, 0.0)

    for whole in ends + [all_z(0), all_z(1)]:
        whole.wait_send()
    via_sent()
    halo_sent(0)
    halo_sent(1)
    assert (n_send[0], n_recv[0]) == (N_SEND, N_RECV), (n_send, n_recv)


def write_out(band, head, band_out, head_out, sem):
    copies = [
        pltpu.make_async_copy(src, dst, sem.at[i])
        for i, (src, dst) in enumerate(((band, band_out), (head, head_out)))
    ]
    for copy in copies:
        copy.start()
    for copy in copies:
        copy.wait()


N_SEND, N_RECV = 33, 71


def body(
    band_feats,
    head_feats,
    mix_weights,
    tile_place,
    tile_vals,
    arrow_cols,
    arrow_reach,
    arrow_rows,
    band_degree,
    head_degree,
):
    rows, width = band_feats.shape
    heads = arrow_rows.shape[0]
    piece = heads // (NZ * NX)
    vmem = pl.BlockSpec(memory_space=pltpu.VMEM)
    hbm = pl.BlockSpec(memory_space=pl.ANY)
    results = pl.pallas_call(
        kernel,
        out_shape=(pltpu.VMEM((rows, width), F32), pltpu.VMEM(head_feats.shape, F32)),
        in_specs=[hbm] * 10,
        out_specs=(vmem, vmem),
        scratch_shapes=[
            pltpu.VMEM(tile_place.shape[::-1], jnp.int32),
            pltpu.VMEM((rows // TILE, TILE), jnp.int32),
            pltpu.VMEM((heads // TILE, TILE), jnp.int32),
            pltpu.VMEM((rows // TILE, TILE), jnp.int32),
            pltpu.VMEM((rows, width), F32),
            pltpu.VMEM(mix_weights.shape, BF16),
            pltpu.VMEM((tile_vals.shape[0] + 1, TILE, TILE), BF16),
            pltpu.VMEM(arrow_cols.shape, BF16),
            pltpu.VMEM(arrow_rows.shape, BF16),
            pltpu.VMEM(arrow_rows.shape, BF16),
            pltpu.VMEM((rows, 3 * rows), BF16),
            pltpu.VMEM((2, NL * NC, rows, width), BF16),
            pltpu.VMEM((2, 3 * rows, width), BF16),
            pltpu.VMEM((rows, width), F32),
            pltpu.VMEM((NX, heads // NX, width), F32),
            pltpu.VMEM((2, NX, heads // NX, width), BF16),
            pltpu.VMEM((2, NX - 1, heads // NX, width), BF16),
            pltpu.VMEM((2, NZ, piece, width), BF16),
            pltpu.VMEM((2, NZ - 1, piece, width), BF16),
            pltpu.VMEM((piece, width), BF16),
            pltpu.VMEM((NY - 1, piece, width), BF16),
            pltpu.VMEM((NY, *head_feats.shape), F32),
            pltpu.VMEM((NY - 1, *head_feats.shape), F32),
            pltpu.VMEM((NL * NC, *head_feats.shape), F32),
            pltpu.VMEM((2, NL * NC, piece, width), BF16),
            pltpu.VMEM((NL * NC, *head_feats.shape), F32),
            pltpu.VMEM((NX, head_feats.shape[0], width // 2), F32),
            pltpu.VMEM((2, len(RELAYED), rows // CHUNKS, width), BF16),
            pltpu.VMEM((len(VIA), rows // CHUNKS, width), BF16),
            pltpu.VMEM((2, NZ, NX, piece, width // 2), BF16),
            pltpu.VMEM((NZ, head_feats.shape[0], width // 2), F32),
            pltpu.VMEM((2, NX, heads // NX, width // 2), BF16),
            pltpu.VMEM(arrow_cols.shape, BF16),
            pltpu.VMEM((heads // NX, TILE), F32),
            pltpu.VMEM((rows, TILE), F32),
            pltpu.VMEM((8, TILE), jnp.int32),
            pltpu.SMEM((8, TILE), jnp.int32),
            pltpu.SemaphoreType.DMA((12,)),
            pltpu.SemaphoreType.DMA((N_SEND,)),
            pltpu.SemaphoreType.DMA((N_RECV,)),
        ],
        compiler_params=pltpu.CompilerParams(collective_id=0, has_side_effects=True),
    )(
        tile_place.T,
        band_degree.reshape(-1, TILE),
        head_degree.reshape(-1, TILE),
        arrow_reach.reshape(-1, TILE),
        band_feats,
        head_feats,
        mix_weights,
        tile_vals,
        arrow_cols,
        arrow_rows,
    )
    return pl.pallas_call(
        write_out,
        out_shape=(
            jax.ShapeDtypeStruct((rows, width), F32),
            jax.ShapeDtypeStruct(head_feats.shape, F32),
        ),
        in_specs=[vmem, vmem],
        out_specs=(hbm, hbm),
        scratch_shapes=[pltpu.SemaphoreType.DMA((2,))],
    )(*(pltpu.with_memory_space_constraint(r, pltpu.VMEM) for r in results))


def solution(mesh):
    split = Mesh(
        mesh.devices.reshape(NZ, NY, NX, NL, NC), (*ROWS, *FEAT)
    )
    return jax.shard_map(
        body,
        mesh=split,
        in_specs=(
            P(ROWS, FEAT),
            P(ROWS, FEAT),
            P(None, None, FEAT),
            P(ROWS, None),
            P(ROWS, None, None),
            P(ROWS, None),
            P(ROWS),
            P(None, ROWS),
            P(ROWS),
            P(),
        ),
        out_specs=(P(ROWS, FEAT), P(ROWS, FEAT)),
        check_vma=False,
    )
```

```python
import functools

import jax
import jax.numpy as jnp
from jax import lax
from jax.experimental import pallas as pl
from jax.experimental.pallas import tpu as pltpu
from jax.sharding import Mesh
from jax.sharding import PartitionSpec as P

MESH = pl.DeviceIdType.MESH
F32, BF16 = jnp.float32, jnp.bfloat16
NZ, NY, NX, NL, NC = 8, 4, 4, 2, 2
ROWS = ("z", "yh", "x")
FEAT = ("yl", "core")
TILE = 128
CHUNKS = 8
RELAYED = (0, 1, 2, 4)
VIA = (6, 7)


def dot(a, b):
    return jnp.dot(a, b, preferred_element_type=F32)


def down_rows(line):
    return jnp.broadcast_to(line, (TILE, line.shape[-1])).T


def kernel(
    place_hbm,
    deg_hbm,
    hdeg_hbm,
    reach_hbm,
    x_hbm,
    h_hbm,
    w_hbm,
    t_hbm,
    c_hbm,
    r_hbm,
    band_out,
    head_out,
    place,
    deg,
    hdeg,
    reach,
    xin,
    wts,
    tiles,
    cols,
    rws,
    rws_p,
    dense,
    gath,
    win,
    acc,
    part,
    part_b,
    xrcv,
    zsrc,
    zrcv,
    ysrc,
    yrcv,
    yout,
    yown,
    hf_last,
    feat_h,
    hf,
    h4,
    relay,
    through,
    head,
    half4,
    half_b,
    cols_p,
    hscale,
    bscale,
    lines,
    table,
    lsem,
    ssem,
    rsem,
):
    z, yh, x = (lax.axis_index(a) for a in ROWS)
    yl, core = (lax.axis_index(a) for a in FEAT)
    rank = (z * NY + yh) * NX + x
    me_f = yl * NC + core
    rows = xin.shape[0]
    step_rows = rows // CHUNKS
    tile_rows = rows // TILE
    has_left, has_right = rank > 0, rank < NZ * NY * NX - 1

    def at_rank(r):
        return {"z": r // (NY * NX), "yh": (r // NX) % NY, "x": r % NX}

    left = at_rank(jnp.maximum(rank - 1, 0))
    right = at_rank(jnp.minimum(rank + 1, NZ * NY * NX - 1))
    z_order, y_order, x_order = [4, 3, 5, 2, 6, 1, 7], [2, 1, 3], [2, 1, 3]
    z_peers = {k: {"z": (z + k) % NZ} for k in z_order}
    y_peers = {k: {"yh": (yh + k) % NY} for k in y_order}
    x_peers = {k: {"x": (x + k) % NX} for k in x_order}
    last_x = NX - 1
    below, above = rank >= NX, rank < NZ * NY * NX - NX
    first_col, last_col = x == 0, x == last_x
    relay_right = jnp.logical_and(last_col, has_right)
    relay_left = jnp.logical_and(first_col, has_left)
    serve_right = jnp.logical_and(first_col, above)
    serve_left = jnp.logical_and(last_col, below)
    up = at_rank(jnp.minimum(rank + NX, NZ * NY * NX - 1))
    down = at_rank(jnp.maximum(rank - NX, 0))
    at_first, at_last = {"x": 0 * x}, {"x": 0 * x + last_x}
    corner = jnp.logical_or(first_col, last_col)
    inner = jnp.logical_not(corner)
    beside = {"x": x + 1 - 2 * (x % 2)}
    beyond = {"x": x + 1 - 2 * (x % 2), "yl": 1 - yl}
    greet_up, greet_down = jnp.logical_and(corner, above), jnp.logical_and(corner, below)
    mate = {"core": 1 - core}
    across = {"yl": 1 - yl}
    f_peers = [across, {"yl": 1 - yl, "core": 1 - core}, mate]
    far_slot = (1 - yl) * NC + core

    n_send, n_recv, ends = [0], [0], []

    def fresh(count):
        count[0] += 1
        return count[0] - 1

    def copy_of(src, dst, device, s, r):
        return pltpu.make_async_remote_copy(
            src_ref=src,
            dst_ref=dst,
            send_sem=ssem.at[s],
            recv_sem=rsem.at[r],
            device_id=device,
            device_id_type=MESH,
        )

    def whole_of(like, s, r):
        return copy_of(like, like, mate, s, r)

    def group(like, copies):
        s, r = fresh(n_send), fresh(n_recv)
        for src, dst, device in copies:
            copy_of(src, dst, device, s, r).start()
        whole = whole_of(like, s, r)
        ends.append(whole)
        return [whole]

    def push(src, dst, device, s):
        copy = copy_of(src, dst, device, s, fresh(n_recv))
        copy.start()
        return copy

    shared = {}

    def shared_send(name, step, like):
        if (name, step) not in shared:
            shared[name, step] = fresh(n_send)
            ends.append(whole_of(like, shared[name, step], 0))
        return shared[name, step]

    barrier = pltpu.get_barrier_semaphore()
    greet = [*z_peers.values(), *y_peers.values(), *x_peers.values(), *f_peers, beyond]
    for peer in greet:
        pl.semaphore_signal(barrier, inc=1, device_id=peer, device_id_type=MESH)

    @pl.when(has_left)
    def _():
        pl.semaphore_signal(barrier, inc=1, device_id=left, device_id_type=MESH)

    @pl.when(has_right)
    def _():
        pl.semaphore_signal(barrier, inc=1, device_id=right, device_id_type=MESH)

    @pl.when(greet_up)
    def _():
        pl.semaphore_signal(barrier, inc=1, device_id=up, device_id_type=MESH)

    @pl.when(greet_down)
    def _():
        pl.semaphore_signal(barrier, inc=1, device_id=down, device_id_type=MESH)

    def load(i, src, dst):
        copy = pltpu.make_async_copy(src, dst, lsem.at[i])
        copy.start()
        return copy

    load_x = load(0, x_hbm, xin)
    load_h = load(1, h_hbm, hf.at[me_f])
    load_r = load(2, r_hbm, rws)
    load_x.wait()
    load_w0 = load(3, w_hbm.at[0], wts.at[0])
    load_t = load(4, t_hbm, tiles.at[pl.ds(0, t_hbm.shape[0])])
    load_c = load(5, c_hbm, cols)
    load_w1 = load(6, w_hbm.at[1], wts.at[1])
    load_small = [
        load(8, place_hbm, place),
        load(9, deg_hbm, deg),
        load(10, hdeg_hbm, hdeg),
        load(11, reach_hbm, reach),
    ]
    gath[0, pl.ds(me_f, 1)] = xin[...].astype(BF16)[None]
    load_h.wait()
    others = [has_left, has_right, greet_up, greet_down]
    pl.semaphore_wait(
        barrier, len(greet) + sum(there.astype(jnp.int32) for there in others)
    )

    def head_partial(step, weights):
        part[...] = dot(weights[...], gath[step, me_f]).reshape(part.shape)
        part_b[step] = part[...].astype(BF16)
        return group(
            xrcv.at[step],
            [(part_b.at[step, (x + k) % NX], xrcv.at[step, k - 1], x_peers[k]) for k in x_order],
        )

    def x_finish(step, copies):
        total = part[x]
        for copy in copies:
            copy.wait_recv()
        for k in range(1, NX):
            total = total + xrcv[step, k - 1].astype(F32)
        zsrc[step] = total.reshape(NZ, -1, total.shape[-1]).astype(BF16)
        return group(
            zrcv.at[step],
            [(zsrc.at[step, (z + k) % NZ], zrcv.at[step, k - 1], z_peers[k]) for k in z_order],
        )

    def z_finish(step, copies):
        for copy in copies:
            copy.wait_recv()
        total = zsrc[step, z].astype(F32)
        for k in range(1, NZ):
            total = total + zrcv[step, k - 1].astype(F32)
        if step:
            per = head_out.shape[0]
            for k in range(NY):
                yout[k] = total[k * per : (k + 1) * per]
            return group(
                yown, [(yout.at[(yh + k) % NY], yown.at[k - 1], y_peers[k]) for k in y_order]
            )
        ysrc[...] = total.astype(BF16)
        return group(yrcv, [(ysrc, yrcv.at[k - 1], y_peers[k]) for k in y_order])

    def y_finish(step, copies):
        for copy in copies:
            copy.wait_recv()
        if step:
            return yout[yh] + sum(yown[k] for k in range(NY - 1))
        return ysrc[...].astype(F32) + sum(yrcv[k].astype(F32) for k in range(NY - 1))

    def last_start(value):
        hf_last[me_f] = value
        return spread_f(hf_last)

    def spread_f(ref):
        return group(
            ref.at[pl.ds(0, len(f_peers))], [(ref.at[me_f], ref.at[me_f], peer) for peer in f_peers]
        )

    def last_finish(copies):
        for copy in copies:
            copy.wait_recv()
        width = hf_last.shape[-1]
        return sum(
            dot(hf_last[f].astype(BF16), wts[1, f * width : (f + 1) * width, :])
            for f in range(NL * NC)
        )

    def feat_start(i, value):
        feat_h[i, pl.ds(me_f, 1)] = value.astype(BF16)[None]
        return spread_f(feat_h.at[i])

    def feat_finish(i, step, copies):
        for copy in copies:
            copy.wait_recv()
        width = feat_h.shape[-1]
        return sum(
            dot(feat_h[i, f], wts[step, f * width : (f + 1) * width, :]) for f in range(NL * NC)
        )

    vias = []
    via_s, via_r = fresh(n_send), fresh(n_recv)
    all_vias = whole_of(through, via_s, via_r)

    def over_send(step, i):
        part_of = gath.at[step, me_f, pl.ds(i * step_rows, step_rows)]
        s = shared_send("over", step, gath.at[step, 0])
        if step or i not in VIA:
            return push(part_of, part_of, across, s)
        spare = through.at[VIA.index(i)]
        r = fresh(n_recv)
        straight = copy_of(part_of, part_of, across, s, r)
        beside_copy = copy_of(part_of, spare, beside, s, via_r)
        vias.append(copy_of(spare, part_of, beyond, via_s, r))

        @pl.when(corner)
        def _():
            beside_copy.start()

        @pl.when(inner)
        def _():
            straight.start()

        return straight

    def cross_on():
        @pl.when(inner)
        def _():
            all_vias.wait_recv()
            for onward in vias:
                onward.start()

    def via_sent():
        @pl.when(inner)
        def _():
            all_vias.wait_send()

    def gather_start(step, ahead):
        over = [over_send(step, i) for i in range(ahead)]
        mine = gath.at[step, me_f]
        return group(mine, [(mine, mine, mate)])[0], over

    def hand_on(step, over, i):
        over[i].wait_recv()
        came = gath.at[step, far_slot, pl.ds(i * step_rows, step_rows)]
        return push(came, came, mate, shared_send("hand", step, gath.at[step, 0]))

    halo_sems = [[fresh(n_send) for _i in range(3)] + [fresh(n_recv) for _i in range(2)] for _j in range(2)]

    def mix(step, i):
        width = gath.shape[-1]
        at = slice(i * step_rows, (i + 1) * step_rows)
        mixed = sum(
            dot(gath[step, f, at, :], wts[step, f * width : (f + 1) * width, :])
            for f in range(NL * NC)
        ).astype(BF16)
        win[step, rows + i * step_rows : rows + (i + 1) * step_rows, :] = mixed
        src = win.at[step, pl.ds(rows + i * step_rows, step_rows)]
        to_left_part = win.at[step, pl.ds(i * step_rows, step_rows)]
        to_right_part = win.at[step, pl.ds(2 * rows + i * step_rows, step_rows)]
        s_right, s_left, s_pass, r_right, r_left = halo_sems[step]
        to_right = copy_of(src, to_left_part, right, s_right, r_right)
        to_left = copy_of(src, to_right_part, left, s_left, r_left)
        if i not in RELAYED:

            @pl.when(has_right)
            def _():
                to_right.start()

            @pl.when(has_left)
            def _():
                to_left.start()

            return to_right, to_left, None

        spare = relay.at[step, RELAYED.index(i)]
        r_spare = fresh(n_recv)
        by_first = copy_of(src, spare, at_first, s_right, r_spare)
        by_last = copy_of(src, spare, at_last, s_left, r_spare)
        pass_right = copy_of(spare, to_left_part, up, s_pass, r_right)
        pass_left = copy_of(spare, to_right_part, down, s_pass, r_left)

        @pl.when(relay_right)
        def _():
            by_first.start()

        @pl.when(jnp.logical_and(has_right, jnp.logical_not(last_col)))
        def _():
            to_right.start()

        @pl.when(relay_left)
        def _():
            by_last.start()

        @pl.when(jnp.logical_and(has_left, jnp.logical_not(first_col)))
        def _():
            to_left.start()

        return to_right, to_left, (by_first, by_last, pass_right, pass_left)

    def relay_on(copies):
        by_first, by_last, pass_right, pass_left = copies[2]

        @pl.when(serve_right)
        def _():
            by_first.wait_recv()
            pass_right.start()

        @pl.when(serve_left)
        def _():
            by_last.wait_recv()
            pass_left.start()

    def halo_whole(step):
        s_right, s_left, s_pass, r_right, r_left = halo_sems[step]
        block = win.at[step, pl.ds(0, rows)]
        return (
            whole_of(block, s_right, r_right),
            whole_of(block, s_left, r_left),
            whole_of(relay.at[step], s_pass, r_left),
        )

    def halo_finish(step):
        rightward, leftward, _unused = halo_whole(step)

        @pl.when(has_left)
        def _():
            rightward.wait_recv()

        @pl.when(has_right)
        def _():
            leftward.wait_recv()

    def halo_sent(step):
        rightward, leftward, passed = halo_whole(step)

        @pl.when(has_right)
        def _():
            rightward.wait_send()

        @pl.when(has_left)
        def _():
            leftward.wait_send()

        @pl.when(jnp.logical_or(serve_right, serve_left))
        def _():
            passed.wait_send()

    piece = head.shape[-2]
    half = head.shape[-1]

    z_sems = [(fresh(n_send), fresh(n_recv)) for _i in range(2)]

    def all_z(step):
        return whole_of(head.at[step, pl.ds(0, NZ - 1)], *z_sems[step])

    def hand_z(step, src):
        for k in z_order:
            copy_of(src, src, z_peers[k], *z_sems[step]).start()

    def spread(step, src, peers):
        s = shared_send("head", step, head.at[step, 0, pl.ds(0, len(peers))])
        along = {k: push(src, src, peer, s) for k, peer in peers.items()}
        hand_z(step, src)
        return along

    def spread_y(value):
        head[0, z, yh] = value.astype(BF16)
        return spread(0, head.at[0, z, yh], y_peers)

    def hand_y(along_y):
        for k in (1, 3, 2):
            along_y[k].wait_recv()
            hand_z(0, head.at[0, z, (yh + NY - k) % NY])

    def second_y(copies):
        for copy in copies:
            copy.wait_recv()
        lines = jnp.concatenate([half4[i] for i in range(NZ)], axis=0)
        per = lines.shape[0]
        at = pl.ds(pl.multiple_of(yh * per, per), per)
        half_b[0, x, at] = lines.astype(BF16)
        src = half_b.at[0, x, at]
        return group(
            half_b.at[0, 0, pl.ds(0, (NY - 1) * per)], [(src, src, y_peers[k]) for k in y_order]
        )

    def second_x(step, copies):
        for copy in copies:
            copy.wait_recv()
        src = half_b.at[step, x]
        return group(half_b.at[step, pl.ds(0, NX - 1)], [(src, src, x_peers[k]) for k in x_order])

    def spread_x(value):
        head[1, z, x] = value[:, :half].astype(BF16)
        at = pl.ds(pl.multiple_of(z * piece, piece), piece)
        half_b[1, x, at] = value[:, half:].astype(BF16)
        src = half_b.at[1, x, at]
        second = group(
            half_b.at[1, 0, pl.ds(0, (NZ - 1) * piece)], [(src, src, z_peers[k]) for k in z_order]
        )
        return spread(1, head.at[1, z, x], x_peers), second

    def hand_x(along_x):
        for k in (1, 3, 2):
            along_x[k].wait_recv()
            hand_z(1, head.at[1, z, (x + NX - k) % NX])

    def head_band(step, along_x):
        all_z(step).wait_recv()
        if step:
            first = jnp.concatenate([head[1, :, k].reshape(-1, half) for k in range(NX)])
        else:
            first = head[0].reshape(-1, half)
        one = dot(cols[...], first)
        for copy in along_x:
            copy.wait_recv()
        by = cols if step else cols_p
        two = dot(by[...], half_b[step].reshape(-1, half))
        return jnp.concatenate([one, two], axis=1)

    def permute_cols():
        per = head_out.shape[0]
        for g in range(NX):
            shape = (cols.shape[1], part.shape[1])
            come = lax.broadcasted_iota(jnp.int32, shape, 0)
            to = lax.broadcasted_iota(jnp.int32, shape, 1)
            row = (to // per) % NZ * (NY * NX * per) + to // (NZ * per) * (NX * per)
            pick = jnp.where(come == row + g * per + to % per, 1.0, 0.0).astype(BF16)
            cols_p[:, g * shape[1] : (g + 1) * shape[1]] = dot(cols[...], pick).astype(BF16)

    n_tiles = place.shape[1]
    n_cols = 3 * tile_rows

    def tables():
        tile_row, tile_col, offset = (place[i : i + 1, :] for i in range(3))
        lines[...] = jnp.full(lines.shape, -1, jnp.int32)
        lines[0:1, :n_tiles] = tile_row * n_cols + (offset + 1) * tile_rows + tile_col
        line = lines[0:1, :]
        down = down_rows(line)[:n_tiles]
        slot = lax.broadcasted_iota(jnp.int32, down.shape, 0)
        lane = lax.broadcasted_iota(jnp.int32, down.shape, 1)
        later = jnp.where(jnp.logical_and(down == line, slot > lane), slot, n_tiles)
        first = jnp.where(down == lane, slot, n_tiles)
        lines[0:1, :] = jnp.min(later, axis=0, keepdims=True)
        lines[1:2, :] = jnp.min(first, axis=0, keepdims=True)
        copy = pltpu.make_async_copy(lines, table, lsem.at[7])
        copy.start()
        tiles[n_tiles] = jnp.zeros((TILE, TILE), BF16)
        return copy

    def build():
        for s in reversed(range(n_tiles - 1)):
            tiles[s] = tiles[s] + tiles[table[0, s]]
        for c in range(tile_rows * n_cols):
            r, w = c // n_cols, c % n_cols
            dense[r * TILE : (r + 1) * TILE, w * TILE : (w + 1) * TILE] = tiles[table[1, c]]

    def edges():
        @pl.when(jnp.logical_not(has_left))
        def _():
            for step in range(2):
                win[step, :rows] = jnp.zeros((rows, win.shape[-1]), BF16)

        @pl.when(jnp.logical_not(has_right))
        def _():
            for step in range(2):
                win[step, 2 * rows :] = jnp.zeros((rows, win.shape[-1]), BF16)

    def mask_cols(i):
        at = slice(i * TILE, (i + 1) * TILE)
        limit = down_rows(reach[i : i + 1, :])
        bscale[at, :] = lax.rsqrt(down_rows(deg[i : i + 1, :].astype(F32)))
        for j in range(cols.shape[1] // TILE):
            lane = lax.broadcasted_iota(jnp.int32, (TILE, TILE), 1) + j * TILE
            block = cols[at, j * TILE : (j + 1) * TILE]
            cols[at, j * TILE : (j + 1) * TILE] = jnp.where(
                lane < limit, block.astype(F32), 0.0
            ).astype(BF16)

    def permute_rows():
        per = head_out.shape[0]
        for g in range(NX):
            shape = (part.shape[1], rws.shape[0])
            to = lax.broadcasted_iota(jnp.int32, shape, 0)
            come = lax.broadcasted_iota(jnp.int32, shape, 1)
            source = (to // per) * (NX * per) + g * per + to % per
            pick = jnp.where(come == source, 1.0, 0.0).astype(BF16)
            rws_p[g * shape[0] : (g + 1) * shape[0], :] = dot(pick, rws[...]).astype(BF16)

    def own_band(step):
        acc[...] = dot(dense[:, rows : 2 * rows], win[step, rows : 2 * rows, :])

    def halo_band(step):
        acc[...] += dot(dense[:, :rows], win[step, :rows, :]) + dot(
            dense[:, 2 * rows :], win[step, 2 * rows :, :]
        )

    def state(step, along_x):
        from_head = head_band(step, along_x)
        scale = jnp.concatenate([bscale[...], bscale[...]], axis=1)
        return jnp.maximum((acc[...] + from_head) * scale, 0.0)

    heads_f = spread_f(hf)
    own0, over0 = gather_start(0, CHUNKS)
    load_r.wait()
    x0 = head_partial(0, rws)
    for copy in load_small:
        copy.wait()
    tabled = tables()
    for copy in heads_f:
        copy.wait_recv()
    load_w0.wait()
    width = hf.shape[-1]
    own_rows = sum(
        dot(hf[f].astype(BF16), wts[0, f * width : (f + 1) * width, :]) for f in range(NL * NC)
    )
    h4[x] = own_rows[:, :half]
    half4[z] = own_rows[:, half:]
    heads_x = group(h4.at[pl.ds(0, NX - 1)], [(h4.at[x], h4.at[x], x_peers[k]) for k in x_order])
    second = group(
        half4.at[pl.ds(0, NZ - 1)], [(half4.at[z], half4.at[z], z_peers[k]) for k in z_order]
    )
    hand0, halo0 = [], []

    def mix_next(step, over, hand, halo):
        if len(hand) < CHUNKS:
            hand.append(hand_on(step, over, len(hand)))
        hand[len(halo)].wait_recv()
        halo.append(mix(step, len(halo)))

    cross_on()
    hand0.append(hand_on(0, over0, 0))
    own0.wait_recv()
    mix_next(0, over0, hand0, halo0)
    mix_next(0, over0, hand0, halo0)
    mix_next(0, over0, hand0, halo0)
    for copy in heads_x:
        copy.wait_recv()
    along_y = spread_y(jnp.concatenate([h4[k] for k in range(NX)], axis=0))
    mix_next(0, over0, hand0, halo0)
    mix_next(0, over0, hand0, halo0)
    second = second_y(second)
    z0 = x_finish(0, x0)
    relay_on(halo0[0])
    mix_next(0, over0, hand0, halo0)
    relay_on(halo0[1])
    mix_next(0, over0, hand0, halo0)
    relay_on(halo0[2])
    mix_next(0, over0, hand0, halo0)
    load_t.wait()
    tabled.wait()
    build()
    relay_on(halo0[4])
    hand_y(along_y)
    edges()
    own_band(0)
    second = second_x(0, second)
    y0 = z_finish(0, z0)
    load_c.wait()
    for i in range(tile_rows):
        mask_cols(i)
    permute_cols()
    permute_rows()
    hscale[...] = lax.rsqrt(down_rows(hdeg[pl.ds(x, 1), :].astype(F32)))
    h_scale = hscale[pl.ds(pl.multiple_of(z * piece, piece), piece), :]
    h_scale = jnp.concatenate([h_scale, h_scale], axis=1)
    halo_finish(0)
    halo_band(0)
    gath[1, pl.ds(me_f, 1)] = state(0, second).astype(BF16)[None]
    feat_b = feat_start(0, y_finish(0, y0))
    own1, over1 = gather_start(1, CHUNKS)
    x1 = head_partial(1, rws_p)
    load_w1.wait()
    hand1, halo1 = [hand_on(1, over1, 0)], []
    own1.wait_recv()
    mix_next(1, over1, hand1, halo1)
    h1 = jnp.maximum(feat_finish(0, 0, feat_b) * h_scale, 0.0)
    feat_c = feat_start(1, h1)
    mix_next(1, over1, hand1, halo1)
    z1 = x_finish(1, x1)
    for _i in range(3):
        mix_next(1, over1, hand1, halo1)
    along_x, second = spread_x(feat_finish(1, 1, feat_c))
    mix_next(1, over1, hand1, halo1)
    relay_on(halo1[0])
    mix_next(1, over1, hand1, halo1)
    relay_on(halo1[1])
    mix_next(1, over1, hand1, halo1)
    relay_on(halo1[2])
    hand_x(along_x)
    y1 = z_finish(1, z1)
    relay_on(halo1[4])
    second = second_x(1, second)
    own_band(1)
    feat_d = last_start(y_finish(1, y1))
    halo_finish(1)
    halo_band(1)
    band_out[...] = state(1, second)
    sums = last_finish(feat_d)
    per = head_out.shape[0]
    near_z = hscale.shape[0] // (per * NX * NY)
    hscale[...] = lax.rsqrt(down_rows(hdeg[pl.ds(z // near_z, 1), :].astype(F32)))
    at = pl.multiple_of((z % near_z) * NY * NX * per + yh * NX * per, NX * per)
    near = hscale[pl.ds(at, NX * per), :]
    near = jnp.concatenate([near, near], axis=1)
    own_scale = jnp.zeros(head_out.shape, F32)
    for k in range(NX):
        own_scale = own_scale + jnp.where(x == k, near[k * per : (k + 1) * per, :], 0.0)
    head_out[...] = jnp.maximum(sums * own_scale, 0.0)

    for whole in ends + [all_z(0), all_z(1)]:
        whole.wait_send()
    via_sent()
    halo_sent(0)
    halo_sent(1)
    assert (n_send[0], n_recv[0]) == (N_SEND, N_RECV), (n_send, n_recv)


def write_out(band, head, band_out, head_out, sem):
    copies = [
        pltpu.make_async_copy(src, dst, sem.at[i])
        for i, (src, dst) in enumerate(((band, band_out), (head, head_out)))
    ]
    for copy in copies:
        copy.start()
    for copy in copies:
        copy.wait()


N_SEND, N_RECV = 33, 71


def body(
    band_feats,
    head_feats,
    mix_weights,
    tile_place,
    tile_vals,
    arrow_cols,
    arrow_reach,
    arrow_rows,
    band_degree,
    head_degree,
):
    rows, width = band_feats.shape
    heads = arrow_rows.shape[0]
    piece = heads // (NZ * NX)
    vmem = pl.BlockSpec(memory_space=pltpu.VMEM)
    hbm = pl.BlockSpec(memory_space=pl.ANY)
    results = pl.pallas_call(
        kernel,
        out_shape=(pltpu.VMEM((rows, width), F32), pltpu.VMEM(head_feats.shape, F32)),
        in_specs=[hbm] * 10,
        out_specs=(vmem, vmem),
        scratch_shapes=[
            pltpu.VMEM(tile_place.shape[::-1], jnp.int32),
            pltpu.VMEM((rows // TILE, TILE), jnp.int32),
            pltpu.VMEM((heads // TILE, TILE), jnp.int32),
            pltpu.VMEM((rows // TILE, TILE), jnp.int32),
            pltpu.VMEM((rows, width), F32),
            pltpu.VMEM(mix_weights.shape, BF16),
            pltpu.VMEM((tile_vals.shape[0] + 1, TILE, TILE), BF16),
            pltpu.VMEM(arrow_cols.shape, BF16),
            pltpu.VMEM(arrow_rows.shape, BF16),
            pltpu.VMEM(arrow_rows.shape, BF16),
            pltpu.VMEM((rows, 3 * rows), BF16),
            pltpu.VMEM((2, NL * NC, rows, width), BF16),
            pltpu.VMEM((2, 3 * rows, width), BF16),
            pltpu.VMEM((rows, width), F32),
            pltpu.VMEM((NX, heads // NX, width), F32),
            pltpu.VMEM((2, NX, heads // NX, width), BF16),
            pltpu.VMEM((2, NX - 1, heads // NX, width), BF16),
            pltpu.VMEM((2, NZ, piece, width), BF16),
            pltpu.VMEM((2, NZ - 1, piece, width), BF16),
            pltpu.VMEM((piece, width), BF16),
            pltpu.VMEM((NY - 1, piece, width), BF16),
            pltpu.VMEM((NY, *head_feats.shape), F32),
            pltpu.VMEM((NY - 1, *head_feats.shape), F32),
            pltpu.VMEM((NL * NC, *head_feats.shape), F32),
            pltpu.VMEM((2, NL * NC, piece, width), BF16),
            pltpu.VMEM((NL * NC, *head_feats.shape), F32),
            pltpu.VMEM((NX, head_feats.shape[0], width // 2), F32),
            pltpu.VMEM((2, len(RELAYED), rows // CHUNKS, width), BF16),
            pltpu.VMEM((len(VIA), rows // CHUNKS, width), BF16),
            pltpu.VMEM((2, NZ, NX, piece, width // 2), BF16),
            pltpu.VMEM((NZ, head_feats.shape[0], width // 2), F32),
            pltpu.VMEM((2, NX, heads // NX, width // 2), BF16),
            pltpu.VMEM(arrow_cols.shape, BF16),
            pltpu.VMEM((heads // NX, TILE), F32),
            pltpu.VMEM((rows, TILE), F32),
            pltpu.VMEM((8, TILE), jnp.int32),
            pltpu.SMEM((8, TILE), jnp.int32),
            pltpu.SemaphoreType.DMA((12,)),
            pltpu.SemaphoreType.DMA((N_SEND,)),
            pltpu.SemaphoreType.DMA((N_RECV,)),
        ],
        compiler_params=pltpu.CompilerParams(collective_id=0, has_side_effects=True),
    )(
        tile_place.T,
        band_degree.reshape(-1, TILE),
        head_degree.reshape(-1, TILE),
        arrow_reach.reshape(-1, TILE),
        band_feats,
        head_feats,
        mix_weights,
        tile_vals,
        arrow_cols,
        arrow_rows,
    )
    return pl.pallas_call(
        write_out,
        out_shape=(
            jax.ShapeDtypeStruct((rows, width), F32),
            jax.ShapeDtypeStruct(head_feats.shape, F32),
        ),
        in_specs=[vmem, vmem],
        out_specs=(hbm, hbm),
        scratch_shapes=[pltpu.SemaphoreType.DMA((2,))],
    )(*(pltpu.with_memory_space_constraint(r, pltpu.VMEM) for r in results))


def solution(mesh):
    split = Mesh(
        mesh.devices.reshape(NZ, NY, NX, NL, NC), (*ROWS, *FEAT)
    )
    return jax.shard_map(
        body,
        mesh=split,
        in_specs=(
            P(ROWS, FEAT),
            P(ROWS, FEAT),
            P(None, None, FEAT),
            P(ROWS, None),
            P(ROWS, None, None),
            P(ROWS, None),
            P(ROWS),
            P(None, ROWS),
            P(ROWS),
            P(),
        ),
        out_specs=(P(ROWS, FEAT), P(ROWS, FEAT)),
        check_vma=False,
    )
```

```python
import functools

import jax
import jax.numpy as jnp
from jax import lax
from jax.experimental import pallas as pl
from jax.experimental.pallas import tpu as pltpu
from jax.sharding import Mesh
from jax.sharding import PartitionSpec as P

MESH = pl.DeviceIdType.MESH
F32, BF16 = jnp.float32, jnp.bfloat16
NZ, NY, NX, NL, NC = 8, 4, 4, 2, 2
ROWS = ("z", "yh", "x")
FEAT = ("yl", "core")
TILE = 128
CHUNKS = 8
RELAYED = (0, 1, 2, 4)
VIA = (6, 7)


def dot(a, b):
    return jnp.dot(a, b, preferred_element_type=F32)


def down_rows(line):
    return jnp.broadcast_to(line, (TILE, line.shape[-1])).T


def kernel(
    place_hbm,
    deg_hbm,
    hdeg_hbm,
    reach_hbm,
    x_hbm,
    h_hbm,
    w_hbm,
    t_hbm,
    c_hbm,
    r_hbm,
    band_out,
    head_out,
    place,
    deg,
    hdeg,
    reach,
    xin,
    wts,
    tiles,
    cols,
    rws,
    rws_p,
    dense,
    gath,
    win,
    acc,
    part,
    part_b,
    xrcv,
    zsrc,
    zrcv,
    ysrc,
    yrcv,
    yout,
    yown,
    hf_last,
    feat_h,
    hf,
    h4,
    relay,
    through,
    head,
    half4,
    half_b,
    cols_p,
    hscale,
    bscale,
    lines,
    table,
    lsem,
    ssem,
    rsem,
):
    z, yh, x = (lax.axis_index(a) for a in ROWS)
    yl, core = (lax.axis_index(a) for a in FEAT)
    rank = (z * NY + yh) * NX + x
    me_f = yl * NC + core
    rows = xin.shape[0]
    step_rows = rows // CHUNKS
    tile_rows = rows // TILE
    has_left, has_right = rank > 0, rank < NZ * NY * NX - 1

    def at_rank(r):
        return {"z": r // (NY * NX), "yh": (r // NX) % NY, "x": r % NX}

    left = at_rank(jnp.maximum(rank - 1, 0))
    right = at_rank(jnp.minimum(rank + 1, NZ * NY * NX - 1))
    z_order, y_order, x_order = [4, 3, 5, 2, 6, 1, 7], [2, 1, 3], [2, 1, 3]
    z_peers = {k: {"z": (z + k) % NZ} for k in z_order}
    y_peers = {k: {"yh": (yh + k) % NY} for k in y_order}
    x_peers = {k: {"x": (x + k) % NX} for k in x_order}
    last_x = NX - 1
    below, above = rank >= NX, rank < NZ * NY * NX - NX
    first_col, last_col = x == 0, x == last_x
    relay_right = jnp.logical_and(last_col, has_right)
    relay_left = jnp.logical_and(first_col, has_left)
    serve_right = jnp.logical_and(first_col, above)
    serve_left = jnp.logical_and(last_col, below)
    up = at_rank(jnp.minimum(rank + NX, NZ * NY * NX - 1))
    down = at_rank(jnp.maximum(rank - NX, 0))
    at_first, at_last = {"x": 0 * x}, {"x": 0 * x + last_x}
    corner = jnp.logical_or(first_col, last_col)
    inner = jnp.logical_not(corner)
    beside = {"x": x + 1 - 2 * (x % 2)}
    beyond = {"x": x + 1 - 2 * (x % 2), "yl": 1 - yl}
    greet_up, greet_down = jnp.logical_and(corner, above), jnp.logical_and(corner, below)
    mate = {"core": 1 - core}
    across = {"yl": 1 - yl}
    f_peers = [across, {"yl": 1 - yl, "core": 1 - core}, mate]
    far_slot = (1 - yl) * NC + core

    n_send, n_recv, ends = [0], [0], []

    def fresh(count):
        count[0] += 1
        return count[0] - 1

    def copy_of(src, dst, device, s, r):
        return pltpu.make_async_remote_copy(
            src_ref=src,
            dst_ref=dst,
            send_sem=ssem.at[s],
            recv_sem=rsem.at[r],
            device_id=device,
            device_id_type=MESH,
        )

    def whole_of(like, s, r):
        return copy_of(like, like, mate, s, r)

    def group(like, copies):
        s, r = fresh(n_send), fresh(n_recv)
        for src, dst, device in copies:
            copy_of(src, dst, device, s, r).start()
        whole = whole_of(like, s, r)
        ends.append(whole)
        return [whole]

    def push(src, dst, device, s):
        copy = copy_of(src, dst, device, s, fresh(n_recv))
        copy.start()
        return copy

    shared = {}

    def shared_send(name, step, like):
        if (name, step) not in shared:
            shared[name, step] = fresh(n_send)
            ends.append(whole_of(like, shared[name, step], 0))
        return shared[name, step]

    def load(i, src, dst):
        copy = pltpu.make_async_copy(src, dst, lsem.at[i])
        copy.start()
        return copy

    quarter = rows // 4
    loads_x = []
    for q in range(4):
        at = pl.ds(q * quarter, quarter)
        loads_x.append(load(12 + q, x_hbm.at[at], xin.at[at]))
    load_h = load(1, h_hbm, hf.at[me_f])
    load_r = load(2, r_hbm, rws)

    barrier = pltpu.get_barrier_semaphore()
    greet = [*z_peers.values(), *y_peers.values(), *x_peers.values(), *f_peers, beyond]
    for peer in greet:
        pl.semaphore_signal(barrier, inc=1, device_id=peer, device_id_type=MESH)

    @pl.when(has_left)
    def _():
        pl.semaphore_signal(barrier, inc=1, device_id=left, device_id_type=MESH)

    @pl.when(has_right)
    def _():
        pl.semaphore_signal(barrier, inc=1, device_id=right, device_id_type=MESH)

    @pl.when(greet_up)
    def _():
        pl.semaphore_signal(barrier, inc=1, device_id=up, device_id_type=MESH)

    @pl.when(greet_down)
    def _():
        pl.semaphore_signal(barrier, inc=1, device_id=down, device_id_type=MESH)

    for q, copy in enumerate(loads_x):
        copy.wait()
        at = slice(q * quarter, (q + 1) * quarter)
        gath[0, pl.ds(me_f, 1), at] = xin[at].astype(BF16)[None]
    load_w0 = load(3, w_hbm.at[0], wts.at[0])
    load_t = load(4, t_hbm, tiles.at[pl.ds(0, t_hbm.shape[0])])
    load_c = load(5, c_hbm, cols)
    load_w1 = load(6, w_hbm.at[1], wts.at[1])
    load_small = [
        load(8, place_hbm, place),
        load(9, deg_hbm, deg),
        load(10, hdeg_hbm, hdeg),
        load(11, reach_hbm, reach),
    ]
    load_h.wait()
    others = [has_left, has_right, greet_up, greet_down]
    pl.semaphore_wait(
        barrier, len(greet) + sum(there.astype(jnp.int32) for there in others)
    )

    def head_partial(step, weights):
        part[...] = dot(weights[...], gath[step, me_f]).reshape(part.shape)
        part_b[step] = part[...].astype(BF16)
        return group(
            xrcv.at[step],
            [(part_b.at[step, (x + k) % NX], xrcv.at[step, k - 1], x_peers[k]) for k in x_order],
        )

    def x_finish(step, copies):
        total = part[x]
        for copy in copies:
            copy.wait_recv()
        for k in range(1, NX):
            total = total + xrcv[step, k - 1].astype(F32)
        zsrc[step] = total.reshape(NZ, -1, total.shape[-1]).astype(BF16)
        return group(
            zrcv.at[step],
            [(zsrc.at[step, (z + k) % NZ], zrcv.at[step, k - 1], z_peers[k]) for k in z_order],
        )

    def z_finish(step, copies):
        for copy in copies:
            copy.wait_recv()
        total = zsrc[step, z].astype(F32)
        for k in range(1, NZ):
            total = total + zrcv[step, k - 1].astype(F32)
        if step:
            per = head_out.shape[0]
            for k in range(NY):
                yout[k] = total[k * per : (k + 1) * per]
            return group(
                yown, [(yout.at[(yh + k) % NY], yown.at[k - 1], y_peers[k]) for k in y_order]
            )
        ysrc[...] = total.astype(BF16)
        return group(yrcv, [(ysrc, yrcv.at[k - 1], y_peers[k]) for k in y_order])

    def y_finish(step, copies):
        for copy in copies:
            copy.wait_recv()
        if step:
            return yout[yh] + sum(yown[k] for k in range(NY - 1))
        return ysrc[...].astype(F32) + sum(yrcv[k].astype(F32) for k in range(NY - 1))

    def last_start(value):
        hf_last[me_f] = value
        return spread_f(hf_last)

    def spread_f(ref):
        return group(
            ref.at[pl.ds(0, len(f_peers))], [(ref.at[me_f], ref.at[me_f], peer) for peer in f_peers]
        )

    def last_finish(copies):
        for copy in copies:
            copy.wait_recv()
        width = hf_last.shape[-1]
        return sum(
            dot(hf_last[f].astype(BF16), wts[1, f * width : (f + 1) * width, :])
            for f in range(NL * NC)
        )

    def feat_start(i, value):
        feat_h[i, pl.ds(me_f, 1)] = value.astype(BF16)[None]
        return spread_f(feat_h.at[i])

    def feat_finish(i, step, copies):
        for copy in copies:
            copy.wait_recv()
        width = feat_h.shape[-1]
        return sum(
            dot(feat_h[i, f], wts[step, f * width : (f + 1) * width, :]) for f in range(NL * NC)
        )

    vias = []
    via_s, via_r = fresh(n_send), fresh(n_recv)
    all_vias = whole_of(through, via_s, via_r)

    def over_send(step, i):
        part_of = gath.at[step, me_f, pl.ds(i * step_rows, step_rows)]
        s = shared_send("over", step, gath.at[step, 0])
        if step or i not in VIA:
            return push(part_of, part_of, across, s)
        spare = through.at[VIA.index(i)]
        r = fresh(n_recv)
        straight = copy_of(part_of, part_of, across, s, r)
        beside_copy = copy_of(part_of, spare, beside, s, via_r)
        vias.append(copy_of(spare, part_of, beyond, via_s, r))

        @pl.when(corner)
        def _():
            beside_copy.start()

        @pl.when(inner)
        def _():
            straight.start()

        return straight

    def cross_on():
        @pl.when(inner)
        def _():
            all_vias.wait_recv()
            for onward in vias:
                onward.start()

    def via_sent():
        @pl.when(inner)
        def _():
            all_vias.wait_send()

    def gather_start(step, ahead):
        over = [over_send(step, i) for i in range(ahead)]
        mine = gath.at[step, me_f]
        return group(mine, [(mine, mine, mate)])[0], over

    def hand_on(step, over, i):
        over[i].wait_recv()
        came = gath.at[step, far_slot, pl.ds(i * step_rows, step_rows)]
        return push(came, came, mate, shared_send("hand", step, gath.at[step, 0]))

    halo_sems = [[fresh(n_send) for _i in range(3)] + [fresh(n_recv) for _i in range(2)] for _j in range(2)]

    def mix(step, i):
        width = gath.shape[-1]
        at = slice(i * step_rows, (i + 1) * step_rows)
        mixed = sum(
            dot(gath[step, f, at, :], wts[step, f * width : (f + 1) * width, :])
            for f in range(NL * NC)
        ).astype(BF16)
        win[step, rows + i * step_rows : rows + (i + 1) * step_rows, :] = mixed
        src = win.at[step, pl.ds(rows + i * step_rows, step_rows)]
        to_left_part = win.at[step, pl.ds(i * step_rows, step_rows)]
        to_right_part = win.at[step, pl.ds(2 * rows + i * step_rows, step_rows)]
        s_right, s_left, s_pass, r_right, r_left = halo_sems[step]
        to_right = copy_of(src, to_left_part, right, s_right, r_right)
        to_left = copy_of(src, to_right_part, left, s_left, r_left)
        if i not in RELAYED:

            @pl.when(has_right)
            def _():
                to_right.start()

            @pl.when(has_left)
            def _():
                to_left.start()

            return to_right, to_left, None

        spare = relay.at[step, RELAYED.index(i)]
        r_spare = fresh(n_recv)
        by_first = copy_of(src, spare, at_first, s_right, r_spare)
        by_last = copy_of(src, spare, at_last, s_left, r_spare)
        pass_right = copy_of(spare, to_left_part, up, s_pass, r_right)
        pass_left = copy_of(spare, to_right_part, down, s_pass, r_left)

        @pl.when(relay_right)
        def _():
            by_first.start()

        @pl.when(jnp.logical_and(has_right, jnp.logical_not(last_col)))
        def _():
            to_right.start()

        @pl.when(relay_left)
        def _():
            by_last.start()

        @pl.when(jnp.logical_and(has_left, jnp.logical_not(first_col)))
        def _():
            to_left.start()

        return to_right, to_left, (by_first, by_last, pass_right, pass_left)

    def relay_on(copies):
        by_first, by_last, pass_right, pass_left = copies[2]

        @pl.when(serve_right)
        def _():
            by_first.wait_recv()
            pass_right.start()

        @pl.when(serve_left)
        def _():
            by_last.wait_recv()
            pass_left.start()

    def halo_whole(step):
        s_right, s_left, s_pass, r_right, r_left = halo_sems[step]
        block = win.at[step, pl.ds(0, rows)]
        return (
            whole_of(block, s_right, r_right),
            whole_of(block, s_left, r_left),
            whole_of(relay.at[step], s_pass, r_left),
        )

    def halo_finish(step, side):
        rightward, leftward, _unused = halo_whole(step)
        from_left = first_col if side else jnp.logical_not(first_col)

        @pl.when(jnp.logical_and(has_left, from_left))
        def _():
            rightward.wait_recv()

        @pl.when(jnp.logical_and(has_right, jnp.logical_not(from_left)))
        def _():
            leftward.wait_recv()

    def halo_sent(step):
        rightward, leftward, passed = halo_whole(step)

        @pl.when(has_right)
        def _():
            rightward.wait_send()

        @pl.when(has_left)
        def _():
            leftward.wait_send()

        @pl.when(jnp.logical_or(serve_right, serve_left))
        def _():
            passed.wait_send()

    piece = head.shape[-2]
    half = head.shape[-1]

    z_sems = [(fresh(n_send), fresh(n_recv)) for _i in range(2)]

    def all_z(step):
        return whole_of(head.at[step, pl.ds(0, NZ - 1)], *z_sems[step])

    def hand_z(step, src):
        for k in z_order:
            copy_of(src, src, z_peers[k], *z_sems[step]).start()

    def spread(step, src, peers):
        s = shared_send("head", step, head.at[step, 0, pl.ds(0, len(peers))])
        along = {k: push(src, src, peer, s) for k, peer in peers.items()}
        hand_z(step, src)
        return along

    def spread_y(value):
        head[0, z, yh] = value.astype(BF16)
        return spread(0, head.at[0, z, yh], y_peers)

    def hand_y(along_y):
        for k in (1, 3, 2):
            along_y[k].wait_recv()
            hand_z(0, head.at[0, z, (yh + NY - k) % NY])

    def second_y(copies):
        for copy in copies:
            copy.wait_recv()
        lines = jnp.concatenate([half4[i] for i in range(NZ)], axis=0)
        per = lines.shape[0]
        at = pl.ds(pl.multiple_of(yh * per, per), per)
        half_b[0, x, at] = lines.astype(BF16)
        src = half_b.at[0, x, at]
        return group(
            half_b.at[0, 0, pl.ds(0, (NY - 1) * per)], [(src, src, y_peers[k]) for k in y_order]
        )

    def second_x(step, copies):
        for copy in copies:
            copy.wait_recv()
        src = half_b.at[step, x]
        return group(half_b.at[step, pl.ds(0, NX - 1)], [(src, src, x_peers[k]) for k in x_order])

    def spread_x(value):
        head[1, z, x] = value[:, :half].astype(BF16)
        at = pl.ds(pl.multiple_of(z * piece, piece), piece)
        half_b[1, x, at] = value[:, half:].astype(BF16)
        src = half_b.at[1, x, at]
        second = group(
            half_b.at[1, 0, pl.ds(0, (NZ - 1) * piece)], [(src, src, z_peers[k]) for k in z_order]
        )
        return spread(1, head.at[1, z, x], x_peers), second

    def hand_x(along_x):
        for k in (1, 3, 2):
            along_x[k].wait_recv()
            hand_z(1, head.at[1, z, (x + NX - k) % NX])

    def head_band(step, along_x):
        all_z(step).wait_recv()
        if step:
            first = jnp.concatenate([head[1, :, k].reshape(-1, half) for k in range(NX)])
        else:
            first = head[0].reshape(-1, half)
        one = None if step else dot(cols[...], first)
        for copy in along_x:
            copy.wait_recv()
        other = half_b[step].reshape(-1, half)
        if step:
            return dot(cols[...], jnp.concatenate([first, other], axis=1))
        return jnp.concatenate([one, dot(cols_p[...], other)], axis=1)

    def permute_cols():
        per = head_out.shape[0]
        for g in range(NX):
            shape = (cols.shape[1], part.shape[1])
            come = lax.broadcasted_iota(jnp.int32, shape, 0)
            to = lax.broadcasted_iota(jnp.int32, shape, 1)
            row = (to // per) % NZ * (NY * NX * per) + to // (NZ * per) * (NX * per)
            pick = jnp.where(come == row + g * per + to % per, 1.0, 0.0).astype(BF16)
            cols_p[:, g * shape[1] : (g + 1) * shape[1]] = dot(cols[...], pick).astype(BF16)

    n_tiles = place.shape[1]
    n_cols = 3 * tile_rows

    def tables():
        tile_row, tile_col, offset = (place[i : i + 1, :] for i in range(3))
        lines[...] = jnp.full(lines.shape, -1, jnp.int32)
        lines[0:1, :n_tiles] = tile_row * n_cols + (offset + 1) * tile_rows + tile_col
        line = lines[0:1, :]
        down = down_rows(line)[:n_tiles]
        slot = lax.broadcasted_iota(jnp.int32, down.shape, 0)
        lane = lax.broadcasted_iota(jnp.int32, down.shape, 1)
        later = jnp.where(jnp.logical_and(down == line, slot > lane), slot, n_tiles)
        first = jnp.where(down == lane, slot, n_tiles)
        lines[0:1, :] = jnp.min(later, axis=0, keepdims=True)
        lines[1:2, :] = jnp.min(first, axis=0, keepdims=True)
        copy = pltpu.make_async_copy(lines, table, lsem.at[7])
        copy.start()
        tiles[n_tiles] = jnp.zeros((TILE, TILE), BF16)
        return copy

    def build():
        for s in reversed(range(n_tiles - 1)):
            tiles[s] = tiles[s] + tiles[table[0, s]]
        for c in range(tile_rows * n_cols):
            r, w = c // n_cols, c % n_cols
            dense[r * TILE : (r + 1) * TILE, w * TILE : (w + 1) * TILE] = tiles[table[1, c]]

    def edges():
        @pl.when(jnp.logical_not(has_left))
        def _():
            for step in range(2):
                win[step, :rows] = jnp.zeros((rows, win.shape[-1]), BF16)

        @pl.when(jnp.logical_not(has_right))
        def _():
            for step in range(2):
                win[step, 2 * rows :] = jnp.zeros((rows, win.shape[-1]), BF16)

    def mask_cols(i):
        at = slice(i * TILE, (i + 1) * TILE)
        limit = down_rows(reach[i : i + 1, :])
        bscale[at, :] = lax.rsqrt(down_rows(deg[i : i + 1, :].astype(F32)))
        for j in range(cols.shape[1] // TILE):
            lane = lax.broadcasted_iota(jnp.int32, (TILE, TILE), 1) + j * TILE
            block = cols[at, j * TILE : (j + 1) * TILE]
            cols[at, j * TILE : (j + 1) * TILE] = jnp.where(
                lane < limit, block.astype(F32), 0.0
            ).astype(BF16)

    def permute_rows():
        per = head_out.shape[0]
        for g in range(NX):
            shape = (part.shape[1], rws.shape[0])
            to = lax.broadcasted_iota(jnp.int32, shape, 0)
            come = lax.broadcasted_iota(jnp.int32, shape, 1)
            source = (to // per) * (NX * per) + g * per + to % per
            pick = jnp.where(come == source, 1.0, 0.0).astype(BF16)
            rws_p[g * shape[0] : (g + 1) * shape[0], :] = dot(pick, rws[...]).astype(BF16)

    def own_band(step):
        acc[...] = dot(dense[:, rows : 2 * rows], win[step, rows : 2 * rows, :])

    def halo_side(step, side):
        halo_finish(step, side)
        first = jnp.where(first_col, 2 * rows * (1 - side), 2 * rows * side)
        at = pl.ds(pl.multiple_of(first, rows), rows)
        return dot(dense[:, at], win[step, at, :])

    def state(step, along_x):
        acc[...] += head_band(step, along_x)
        scale = jnp.concatenate([bscale[...], bscale[...]], axis=1)
        return jnp.maximum((acc[...] + halo_side(step, 1)) * scale, 0.0)

    heads_f = spread_f(hf)
    own0, over0 = gather_start(0, CHUNKS)
    load_r.wait()
    x0 = head_partial(0, rws)
    for copy in load_small:
        copy.wait()
    tabled = tables()
    for copy in heads_f:
        copy.wait_recv()
    load_w0.wait()
    width = hf.shape[-1]
    own_rows = sum(
        dot(hf[f].astype(BF16), wts[0, f * width : (f + 1) * width, :]) for f in range(NL * NC)
    )
    h4[x] = own_rows[:, :half]
    half4[z] = own_rows[:, half:]
    heads_x = group(h4.at[pl.ds(0, NX - 1)], [(h4.at[x], h4.at[x], x_peers[k]) for k in x_order])
    second = group(
        half4.at[pl.ds(0, NZ - 1)], [(half4.at[z], half4.at[z], z_peers[k]) for k in z_order]
    )
    hand0, halo0 = [], []

    def mix_next(step, over, hand, halo):
        if len(hand) < CHUNKS:
            hand.append(hand_on(step, over, len(hand)))
        hand[len(halo)].wait_recv()
        halo.append(mix(step, len(halo)))

    cross_on()
    hand0.append(hand_on(0, over0, 0))
    own0.wait_recv()
    mix_next(0, over0, hand0, halo0)
    mix_next(0, over0, hand0, halo0)
    mix_next(0, over0, hand0, halo0)
    for copy in heads_x:
        copy.wait_recv()
    along_y = spread_y(jnp.concatenate([h4[k] for k in range(NX)], axis=0))
    mix_next(0, over0, hand0, halo0)
    mix_next(0, over0, hand0, halo0)
    second = second_y(second)
    z0 = x_finish(0, x0)
    relay_on(halo0[0])
    mix_next(0, over0, hand0, halo0)
    relay_on(halo0[1])
    mix_next(0, over0, hand0, halo0)
    relay_on(halo0[2])
    mix_next(0, over0, hand0, halo0)
    load_t.wait()
    tabled.wait()
    build()
    relay_on(halo0[4])
    hand_y(along_y)
    edges()
    own_band(0)
    second = second_x(0, second)
    y0 = z_finish(0, z0)
    load_c.wait()
    for i in range(tile_rows):
        mask_cols(i)
    permute_cols()
    permute_rows()
    hscale[...] = lax.rsqrt(down_rows(hdeg[pl.ds(x, 1), :].astype(F32)))
    h_scale = hscale[pl.ds(pl.multiple_of(z * piece, piece), piece), :]
    h_scale = jnp.concatenate([h_scale, h_scale], axis=1)
    acc[...] += halo_side(0, 0)
    gath[1, pl.ds(me_f, 1)] = state(0, second).astype(BF16)[None]
    feat_b = feat_start(0, y_finish(0, y0))
    own1, over1 = gather_start(1, CHUNKS)
    x1 = head_partial(1, rws_p)
    load_w1.wait()
    hand1, halo1 = [hand_on(1, over1, 0)], []
    own1.wait_recv()
    mix_next(1, over1, hand1, halo1)
    h1 = jnp.maximum(feat_finish(0, 0, feat_b) * h_scale, 0.0)
    feat_c = feat_start(1, h1)
    mix_next(1, over1, hand1, halo1)
    z1 = x_finish(1, x1)
    for _i in range(3):
        mix_next(1, over1, hand1, halo1)
    along_x, second = spread_x(feat_finish(1, 1, feat_c))
    mix_next(1, over1, hand1, halo1)
    relay_on(halo1[0])
    mix_next(1, over1, hand1, halo1)
    relay_on(halo1[1])
    mix_next(1, over1, hand1, halo1)
    relay_on(halo1[2])
    y1 = z_finish(1, z1)
    hand_x(along_x)
    relay_on(halo1[4])
    second = second_x(1, second)
    own_band(1)
    acc[...] += halo_side(1, 0)
    feat_d = last_start(y_finish(1, y1))
    band_out[...] = state(1, second)
    sums = last_finish(feat_d)
    per = head_out.shape[0]
    near_z = hscale.shape[0] // (per * NX * NY)
    hscale[...] = lax.rsqrt(down_rows(hdeg[pl.ds(z // near_z, 1), :].astype(F32)))
    at = pl.multiple_of((z % near_z) * NY * NX * per + yh * NX * per, NX * per)
    near = hscale[pl.ds(at, NX * per), :]
    near = jnp.concatenate([near, near], axis=1)
    own_scale = jnp.zeros(head_out.shape, F32)
    for k in range(NX):
        own_scale = own_scale + jnp.where(x == k, near[k * per : (k + 1) * per, :], 0.0)
    head_out[...] = jnp.maximum(sums * own_scale, 0.0)

    for whole in ends + [all_z(0), all_z(1)]:
        whole.wait_send()
    via_sent()
    halo_sent(0)
    halo_sent(1)
    assert (n_send[0], n_recv[0]) == (N_SEND, N_RECV), (n_send, n_recv)


def write_out(band, head, band_out, head_out, sem):
    copies = [
        pltpu.make_async_copy(src, dst, sem.at[i])
        for i, (src, dst) in enumerate(((band, band_out), (head, head_out)))
    ]
    for copy in copies:
        copy.start()
    for copy in copies:
        copy.wait()


N_SEND, N_RECV = 33, 71


def body(
    band_feats,
    head_feats,
    mix_weights,
    tile_place,
    tile_vals,
    arrow_cols,
    arrow_reach,
    arrow_rows,
    band_degree,
    head_degree,
):
    rows, width = band_feats.shape
    heads = arrow_rows.shape[0]
    piece = heads // (NZ * NX)
    vmem = pl.BlockSpec(memory_space=pltpu.VMEM)
    hbm = pl.BlockSpec(memory_space=pl.ANY)
    results = pl.pallas_call(
        kernel,
        out_shape=(pltpu.VMEM((rows, width), F32), pltpu.VMEM(head_feats.shape, F32)),
        in_specs=[hbm] * 10,
        out_specs=(vmem, vmem),
        scratch_shapes=[
            pltpu.VMEM(tile_place.shape[::-1], jnp.int32),
            pltpu.VMEM((rows // TILE, TILE), jnp.int32),
            pltpu.VMEM((heads // TILE, TILE), jnp.int32),
            pltpu.VMEM((rows // TILE, TILE), jnp.int32),
            pltpu.VMEM((rows, width), F32),
            pltpu.VMEM(mix_weights.shape, BF16),
            pltpu.VMEM((tile_vals.shape[0] + 1, TILE, TILE), BF16),
            pltpu.VMEM(arrow_cols.shape, BF16),
            pltpu.VMEM(arrow_rows.shape, BF16),
            pltpu.VMEM(arrow_rows.shape, BF16),
            pltpu.VMEM((rows, 3 * rows), BF16),
            pltpu.VMEM((2, NL * NC, rows, width), BF16),
            pltpu.VMEM((2, 3 * rows, width), BF16),
            pltpu.VMEM((rows, width), F32),
            pltpu.VMEM((NX, heads // NX, width), F32),
            pltpu.VMEM((2, NX, heads // NX, width), BF16),
            pltpu.VMEM((2, NX - 1, heads // NX, width), BF16),
            pltpu.VMEM((2, NZ, piece, width), BF16),
            pltpu.VMEM((2, NZ - 1, piece, width), BF16),
            pltpu.VMEM((piece, width), BF16),
            pltpu.VMEM((NY - 1, piece, width), BF16),
            pltpu.VMEM((NY, *head_feats.shape), F32),
            pltpu.VMEM((NY - 1, *head_feats.shape), F32),
            pltpu.VMEM((NL * NC, *head_feats.shape), F32),
            pltpu.VMEM((2, NL * NC, piece, width), BF16),
            pltpu.VMEM((NL * NC, *head_feats.shape), F32),
            pltpu.VMEM((NX, head_feats.shape[0], width // 2), F32),
            pltpu.VMEM((2, len(RELAYED), rows // CHUNKS, width), BF16),
            pltpu.VMEM((len(VIA), rows // CHUNKS, width), BF16),
            pltpu.VMEM((2, NZ, NX, piece, width // 2), BF16),
            pltpu.VMEM((NZ, head_feats.shape[0], width // 2), F32),
            pltpu.VMEM((2, NX, heads // NX, width // 2), BF16),
            pltpu.VMEM(arrow_cols.shape, BF16),
            pltpu.VMEM((heads // NX, TILE), F32),
            pltpu.VMEM((rows, TILE), F32),
            pltpu.VMEM((8, TILE), jnp.int32),
            pltpu.SMEM((8, TILE), jnp.int32),
            pltpu.SemaphoreType.DMA((16,)),
            pltpu.SemaphoreType.DMA((N_SEND,)),
            pltpu.SemaphoreType.DMA((N_RECV,)),
        ],
        compiler_params=pltpu.CompilerParams(collective_id=0, has_side_effects=True),
    )(
        tile_place.T,
        band_degree.reshape(-1, TILE),
        head_degree.reshape(-1, TILE),
        arrow_reach.reshape(-1, TILE),
        band_feats,
        head_feats,
        mix_weights,
        tile_vals,
        arrow_cols,
        arrow_rows,
    )
    return pl.pallas_call(
        write_out,
        out_shape=(
            jax.ShapeDtypeStruct((rows, width), F32),
            jax.ShapeDtypeStruct(head_feats.shape, F32),
        ),
        in_specs=[vmem, vmem],
        out_specs=(hbm, hbm),
        scratch_shapes=[pltpu.SemaphoreType.DMA((2,))],
    )(*(pltpu.with_memory_space_constraint(r, pltpu.VMEM) for r in results))


def solution(mesh):
    split = Mesh(
        mesh.devices.reshape(NZ, NY, NX, NL, NC), (*ROWS, *FEAT)
    )
    return jax.shard_map(
        body,
        mesh=split,
        in_specs=(
            P(ROWS, FEAT),
            P(ROWS, FEAT),
            P(None, None, FEAT),
            P(ROWS, None),
            P(ROWS, None, None),
            P(ROWS, None),
            P(ROWS),
            P(None, ROWS),
            P(ROWS),
            P(),
        ),
        out_specs=(P(ROWS, FEAT), P(ROWS, FEAT)),
        check_vma=False,
    )
```

```python
import functools

import jax
import jax.numpy as jnp
from jax import lax
from jax.experimental import pallas as pl
from jax.experimental.pallas import tpu as pltpu
from jax.sharding import Mesh
from jax.sharding import PartitionSpec as P

MESH = pl.DeviceIdType.MESH
F32, BF16 = jnp.float32, jnp.bfloat16
NZ, NY, NX, NL, NC = 8, 4, 4, 2, 2
ROWS = ("z", "yh", "x")
FEAT = ("yl", "core")
TILE = 128
CHUNKS = 8
RELAYED = (0, 1, 2, 4)
VIA = (6, 7)


def dot(a, b):
    return jnp.dot(a, b, preferred_element_type=F32)


def down_rows(line):
    return jnp.broadcast_to(line, (TILE, line.shape[-1])).T


def kernel(
    place_hbm,
    deg_hbm,
    hdeg_hbm,
    reach_hbm,
    x_hbm,
    h_hbm,
    w_hbm,
    t_hbm,
    c_hbm,
    r_hbm,
    band_out,
    head_out,
    place,
    deg,
    hdeg,
    reach,
    xin,
    wts,
    tiles,
    cols,
    rws,
    rws_p,
    dense,
    gath,
    win,
    acc,
    part,
    part_b,
    xrcv,
    zsrc,
    zrcv,
    ysrc,
    yrcv,
    yout,
    yown,
    hf_last,
    feat_h,
    hf,
    h4,
    relay,
    through,
    head,
    half4,
    half_b,
    cols_p,
    hscale,
    bscale,
    lines,
    table,
    lsem,
    ssem,
    rsem,
):
    z, yh, x = (lax.axis_index(a) for a in ROWS)
    yl, core = (lax.axis_index(a) for a in FEAT)
    rank = (z * NY + yh) * NX + x
    me_f = yl * NC + core
    rows = xin.shape[0]
    step_rows = rows // CHUNKS
    tile_rows = rows // TILE
    has_left, has_right = rank > 0, rank < NZ * NY * NX - 1

    def at_rank(r):
        return {"z": r // (NY * NX), "yh": (r // NX) % NY, "x": r % NX}

    left = at_rank(jnp.maximum(rank - 1, 0))
    right = at_rank(jnp.minimum(rank + 1, NZ * NY * NX - 1))
    z_order, y_order, x_order = [4, 3, 5, 2, 6, 1, 7], [2, 1, 3], [2, 1, 3]
    z_peers = {k: {"z": (z + k) % NZ} for k in z_order}
    y_peers = {k: {"yh": (yh + k) % NY} for k in y_order}
    x_peers = {k: {"x": (x + k) % NX} for k in x_order}
    last_x = NX - 1
    below, above = rank >= NX, rank < NZ * NY * NX - NX
    first_col, last_col = x == 0, x == last_x
    relay_right = jnp.logical_and(last_col, has_right)
    relay_left = jnp.logical_and(first_col, has_left)
    serve_right = jnp.logical_and(first_col, above)
    serve_left = jnp.logical_and(last_col, below)
    up = at_rank(jnp.minimum(rank + NX, NZ * NY * NX - 1))
    down = at_rank(jnp.maximum(rank - NX, 0))
    at_first, at_last = {"x": 0 * x}, {"x": 0 * x + last_x}
    corner = jnp.logical_or(first_col, last_col)
    inner = jnp.logical_not(corner)
    beside = {"x": x + 1 - 2 * (x % 2)}
    beyond = {"x": x + 1 - 2 * (x % 2), "yl": 1 - yl}
    greet_up, greet_down = jnp.logical_and(corner, above), jnp.logical_and(corner, below)
    mate = {"core": 1 - core}
    across = {"yl": 1 - yl}
    f_peers = [across, {"yl": 1 - yl, "core": 1 - core}, mate]
    far_slot = (1 - yl) * NC + core

    n_send, n_recv, ends = [0], [0], []

    def fresh(count):
        count[0] += 1
        return count[0] - 1

    def copy_of(src, dst, device, s, r):
        return pltpu.make_async_remote_copy(
            src_ref=src,
            dst_ref=dst,
            send_sem=ssem.at[s],
            recv_sem=rsem.at[r],
            device_id=device,
            device_id_type=MESH,
        )

    def whole_of(like, s, r):
        return copy_of(like, like, mate, s, r)

    def group(like, copies):
        s, r = fresh(n_send), fresh(n_recv)
        for src, dst, device in copies:
            copy_of(src, dst, device, s, r).start()
        whole = whole_of(like, s, r)
        ends.append(whole)
        return [whole]

    def push(src, dst, device, s):
        copy = copy_of(src, dst, device, s, fresh(n_recv))
        copy.start()
        return copy

    shared = {}

    def shared_send(name, step, like):
        if (name, step) not in shared:
            shared[name, step] = fresh(n_send)
            ends.append(whole_of(like, shared[name, step], 0))
        return shared[name, step]

    def load(i, src, dst):
        copy = pltpu.make_async_copy(src, dst, lsem.at[i])
        copy.start()
        return copy

    quarter = rows // 4
    loads_x = []
    for q in range(4):
        at = pl.ds(q * quarter, quarter)
        loads_x.append(load(12 + q, x_hbm.at[at], xin.at[at]))
    load_h = load(1, h_hbm, hf.at[me_f])
    load_r = load(2, r_hbm, rws)

    barrier = pltpu.get_barrier_semaphore()
    greet = [*z_peers.values(), *y_peers.values(), *x_peers.values(), *f_peers, beyond]
    for peer in greet:
        pl.semaphore_signal(barrier, inc=1, device_id=peer, device_id_type=MESH)

    @pl.when(has_left)
    def _():
        pl.semaphore_signal(barrier, inc=1, device_id=left, device_id_type=MESH)

    @pl.when(has_right)
    def _():
        pl.semaphore_signal(barrier, inc=1, device_id=right, device_id_type=MESH)

    @pl.when(greet_up)
    def _():
        pl.semaphore_signal(barrier, inc=1, device_id=up, device_id_type=MESH)

    @pl.when(greet_down)
    def _():
        pl.semaphore_signal(barrier, inc=1, device_id=down, device_id_type=MESH)

    for q, copy in enumerate(loads_x):
        copy.wait()
        at = slice(q * quarter, (q + 1) * quarter)
        gath[0, pl.ds(me_f, 1), at] = xin[at].astype(BF16)[None]
    load_w0 = load(3, w_hbm.at[0], wts.at[0])
    load_t = load(4, t_hbm, tiles.at[pl.ds(0, t_hbm.shape[0])])
    load_c = load(5, c_hbm, cols)
    load_w1 = load(6, w_hbm.at[1], wts.at[1])
    load_small = [
        load(8, place_hbm, place),
        load(9, deg_hbm, deg),
        load(10, hdeg_hbm, hdeg),
        load(11, reach_hbm, reach),
    ]
    load_h.wait()
    others = [has_left, has_right, greet_up, greet_down]
    pl.semaphore_wait(
        barrier, len(greet) + sum(there.astype(jnp.int32) for there in others)
    )

    def head_partial(step, weights):
        part[...] = dot(weights[...], gath[step, me_f]).reshape(part.shape)
        part_b[step] = part[...].astype(BF16)
        return group(
            xrcv.at[step],
            [(part_b.at[step, (x + k) % NX], xrcv.at[step, k - 1], x_peers[k]) for k in x_order],
        )

    def x_finish(step, copies):
        total = part[x]
        for copy in copies:
            copy.wait_recv()
        for k in range(1, NX):
            total = total + xrcv[step, k - 1].astype(F32)
        zsrc[step] = total.reshape(NZ, -1, total.shape[-1]).astype(BF16)
        return group(
            zrcv.at[step],
            [(zsrc.at[step, (z + k) % NZ], zrcv.at[step, k - 1], z_peers[k]) for k in z_order],
        )

    def z_finish(step, copies):
        for copy in copies:
            copy.wait_recv()
        total = zsrc[step, z].astype(F32)
        for k in range(1, NZ):
            total = total + zrcv[step, k - 1].astype(F32)
        if step:
            per = head_out.shape[0]
            for k in range(NY):
                yout[k] = total[k * per : (k + 1) * per]
            return group(
                yown, [(yout.at[(yh + k) % NY], yown.at[k - 1], y_peers[k]) for k in y_order]
            )
        ysrc[...] = total.astype(BF16)
        return group(yrcv, [(ysrc, yrcv.at[k - 1], y_peers[k]) for k in y_order])

    def y_finish(step, copies):
        for copy in copies:
            copy.wait_recv()
        if step:
            return yout[yh] + sum(yown[k] for k in range(NY - 1))
        return ysrc[...].astype(F32) + sum(yrcv[k].astype(F32) for k in range(NY - 1))

    def last_start(value):
        hf_last[me_f] = value
        return spread_f(hf_last)

    def spread_f(ref):
        return group(
            ref.at[pl.ds(0, len(f_peers))], [(ref.at[me_f], ref.at[me_f], peer) for peer in f_peers]
        )

    def last_finish(copies):
        for copy in copies:
            copy.wait_recv()
        width = hf_last.shape[-1]
        return sum(
            dot(hf_last[f].astype(BF16), wts[1, f * width : (f + 1) * width, :])
            for f in range(NL * NC)
        )

    def feat_start(i, value):
        feat_h[i, pl.ds(me_f, 1)] = value.astype(BF16)[None]
        return spread_f(feat_h.at[i])

    def feat_finish(i, step, copies):
        for copy in copies:
            copy.wait_recv()
        width = feat_h.shape[-1]
        return sum(
            dot(feat_h[i, f], wts[step, f * width : (f + 1) * width, :]) for f in range(NL * NC)
        )

    vias = []
    via_s, via_r = fresh(n_send), fresh(n_recv)
    all_vias = whole_of(through, via_s, via_r)

    def over_send(step, i):
        part_of = gath.at[step, me_f, pl.ds(i * step_rows, step_rows)]
        s = shared_send("over", step, gath.at[step, 0])
        if step or i not in VIA:
            return push(part_of, part_of, across, s)
        spare = through.at[VIA.index(i)]
        r = fresh(n_recv)
        straight = copy_of(part_of, part_of, across, s, r)
        beside_copy = copy_of(part_of, spare, beside, s, via_r)
        vias.append(copy_of(spare, part_of, beyond, via_s, r))

        @pl.when(corner)
        def _():
            beside_copy.start()

        @pl.when(inner)
        def _():
            straight.start()

        return straight

    def cross_on():
        @pl.when(inner)
        def _():
            all_vias.wait_recv()
            for onward in vias:
                onward.start()

    def via_sent():
        @pl.when(inner)
        def _():
            all_vias.wait_send()

    def gather_start(step, ahead):
        over = [over_send(step, i) for i in range(ahead)]
        mine = gath.at[step, me_f]
        return group(mine, [(mine, mine, mate)])[0], over

    def hand_on(step, over, i):
        over[i].wait_recv()
        came = gath.at[step, far_slot, pl.ds(i * step_rows, step_rows)]
        return push(came, came, mate, shared_send("hand", step, gath.at[step, 0]))

    halo_sems = [[fresh(n_send) for _i in range(3)] + [fresh(n_recv) for _i in range(2)] for _j in range(2)]

    def mix(step, i):
        width = gath.shape[-1]
        at = slice(i * step_rows, (i + 1) * step_rows)
        mixed = sum(
            dot(gath[step, f, at, :], wts[step, f * width : (f + 1) * width, :])
            for f in range(NL * NC)
        ).astype(BF16)
        win[step, rows + i * step_rows : rows + (i + 1) * step_rows, :] = mixed
        src = win.at[step, pl.ds(rows + i * step_rows, step_rows)]
        to_left_part = win.at[step, pl.ds(i * step_rows, step_rows)]
        to_right_part = win.at[step, pl.ds(2 * rows + i * step_rows, step_rows)]
        s_right, s_left, s_pass, r_right, r_left = halo_sems[step]
        to_right = copy_of(src, to_left_part, right, s_right, r_right)
        to_left = copy_of(src, to_right_part, left, s_left, r_left)
        if i not in RELAYED:

            @pl.when(has_right)
            def _():
                to_right.start()

            @pl.when(has_left)
            def _():
                to_left.start()

            return to_right, to_left, None

        spare = relay.at[step, RELAYED.index(i)]
        r_spare = fresh(n_recv)
        by_first = copy_of(src, spare, at_first, s_right, r_spare)
        by_last = copy_of(src, spare, at_last, s_left, r_spare)
        pass_right = copy_of(spare, to_left_part, up, s_pass, r_right)
        pass_left = copy_of(spare, to_right_part, down, s_pass, r_left)

        @pl.when(relay_right)
        def _():
            by_first.start()

        @pl.when(jnp.logical_and(has_right, jnp.logical_not(last_col)))
        def _():
            to_right.start()

        @pl.when(relay_left)
        def _():
            by_last.start()

        @pl.when(jnp.logical_and(has_left, jnp.logical_not(first_col)))
        def _():
            to_left.start()

        return to_right, to_left, (by_first, by_last, pass_right, pass_left)

    def relay_on(copies):
        by_first, by_last, pass_right, pass_left = copies[2]

        @pl.when(serve_right)
        def _():
            by_first.wait_recv()
            pass_right.start()

        @pl.when(serve_left)
        def _():
            by_last.wait_recv()
            pass_left.start()

    def halo_whole(step):
        s_right, s_left, s_pass, r_right, r_left = halo_sems[step]
        block = win.at[step, pl.ds(0, rows)]
        return (
            whole_of(block, s_right, r_right),
            whole_of(block, s_left, r_left),
            whole_of(relay.at[step], s_pass, r_left),
        )

    def halo_finish(step, side):
        rightward, leftward, _unused = halo_whole(step)
        from_left = first_col if side else jnp.logical_not(first_col)

        @pl.when(jnp.logical_and(has_left, from_left))
        def _():
            rightward.wait_recv()

        @pl.when(jnp.logical_and(has_right, jnp.logical_not(from_left)))
        def _():
            leftward.wait_recv()

    def halo_sent(step):
        rightward, leftward, passed = halo_whole(step)

        @pl.when(has_right)
        def _():
            rightward.wait_send()

        @pl.when(has_left)
        def _():
            leftward.wait_send()

        @pl.when(jnp.logical_or(serve_right, serve_left))
        def _():
            passed.wait_send()

    piece = head.shape[-2]
    half = head.shape[-1]

    z_sems = [(fresh(n_send), fresh(n_recv)) for _i in range(2)]

    def all_z(step):
        return whole_of(head.at[step, pl.ds(0, NZ - 1)], *z_sems[step])

    def hand_z(step, src):
        for k in z_order:
            copy_of(src, src, z_peers[k], *z_sems[step]).start()

    def spread(step, src, peers):
        s = shared_send("head", step, head.at[step, 0, pl.ds(0, len(peers))])
        along = {k: push(src, src, peer, s) for k, peer in peers.items()}
        hand_z(step, src)
        return along

    def spread_y(value):
        head[0, z, yh] = value.astype(BF16)
        return spread(0, head.at[0, z, yh], y_peers)

    def hand_y(along_y):
        for k in (1, 3, 2):
            along_y[k].wait_recv()
            hand_z(0, head.at[0, z, (yh + NY - k) % NY])

    def second_y(copies):
        for copy in copies:
            copy.wait_recv()
        lines = jnp.concatenate([half4[i] for i in range(NZ)], axis=0)
        per = lines.shape[0]
        at = pl.ds(pl.multiple_of(yh * per, per), per)
        half_b[0, x, at] = lines.astype(BF16)
        src = half_b.at[0, x, at]
        return group(
            half_b.at[0, 0, pl.ds(0, (NY - 1) * per)], [(src, src, y_peers[k]) for k in y_order]
        )

    def second_x(step, copies):
        for copy in copies:
            copy.wait_recv()
        src = half_b.at[step, x]
        return group(half_b.at[step, pl.ds(0, NX - 1)], [(src, src, x_peers[k]) for k in x_order])

    def spread_x(value):
        head[1, z, x] = value[:, :half].astype(BF16)
        at = pl.ds(pl.multiple_of(z * piece, piece), piece)
        half_b[1, x, at] = value[:, half:].astype(BF16)
        src = half_b.at[1, x, at]
        second = group(
            half_b.at[1, 0, pl.ds(0, (NZ - 1) * piece)], [(src, src, z_peers[k]) for k in z_order]
        )
        return spread(1, head.at[1, z, x], x_peers), second

    def hand_x(along_x):
        for k in (1, 3, 2):
            along_x[k].wait_recv()
            hand_z(1, head.at[1, z, (x + NX - k) % NX])

    def head_band(step, along_x):
        all_z(step).wait_recv()
        if step:
            first = jnp.concatenate([head[1, :, k].reshape(-1, half) for k in range(NX)])
        else:
            first = head[0].reshape(-1, half)
        one = None if step else dot(cols[...], first)
        for copy in along_x:
            copy.wait_recv()
        other = half_b[step].reshape(-1, half)
        if step:
            return dot(cols[...], jnp.concatenate([first, other], axis=1))
        return jnp.concatenate([one, dot(cols_p[...], other)], axis=1)

    def permute_cols():
        per = head_out.shape[0]
        for g in range(NX):
            shape = (cols.shape[1], part.shape[1])
            come = lax.broadcasted_iota(jnp.int32, shape, 0)
            to = lax.broadcasted_iota(jnp.int32, shape, 1)
            row = (to // per) % NZ * (NY * NX * per) + to // (NZ * per) * (NX * per)
            pick = jnp.where(come == row + g * per + to % per, 1.0, 0.0).astype(BF16)
            cols_p[:, g * shape[1] : (g + 1) * shape[1]] = dot(cols[...], pick).astype(BF16)

    n_tiles = place.shape[1]
    n_cols = 3 * tile_rows

    def tables():
        tile_row, tile_col, offset = (place[i : i + 1, :] for i in range(3))
        lines[...] = jnp.full(lines.shape, -1, jnp.int32)
        lines[0:1, :n_tiles] = tile_row * n_cols + (offset + 1) * tile_rows + tile_col
        line = lines[0:1, :]
        down = down_rows(line)[:n_tiles]
        slot = lax.broadcasted_iota(jnp.int32, down.shape, 0)
        lane = lax.broadcasted_iota(jnp.int32, down.shape, 1)
        later = jnp.where(jnp.logical_and(down == line, slot > lane), slot, n_tiles)
        first = jnp.where(down == lane, slot, n_tiles)
        lines[0:1, :] = jnp.min(later, axis=0, keepdims=True)
        lines[1:2, :] = jnp.min(first, axis=0, keepdims=True)
        copy = pltpu.make_async_copy(lines, table, lsem.at[7])
        copy.start()
        tiles[n_tiles] = jnp.zeros((TILE, TILE), BF16)
        return copy

    def build():
        for s in reversed(range(n_tiles - 1)):
            tiles[s] = tiles[s] + tiles[table[0, s]]
        for c in range(tile_rows * n_cols):
            r, w = c // n_cols, c % n_cols
            dense[r * TILE : (r + 1) * TILE, w * TILE : (w + 1) * TILE] = tiles[table[1, c]]

    def edges():
        @pl.when(jnp.logical_not(has_left))
        def _():
            for step in range(2):
                win[step, :rows] = jnp.zeros((rows, win.shape[-1]), BF16)

        @pl.when(jnp.logical_not(has_right))
        def _():
            for step in range(2):
                win[step, 2 * rows :] = jnp.zeros((rows, win.shape[-1]), BF16)

    def mask_cols(i):
        at = slice(i * TILE, (i + 1) * TILE)
        limit = down_rows(reach[i : i + 1, :])
        bscale[at, :] = lax.rsqrt(down_rows(deg[i : i + 1, :].astype(F32)))
        for j in range(cols.shape[1] // TILE):
            lane = lax.broadcasted_iota(jnp.int32, (TILE, TILE), 1) + j * TILE
            block = cols[at, j * TILE : (j + 1) * TILE]
            cols[at, j * TILE : (j + 1) * TILE] = jnp.where(
                lane < limit, block.astype(F32), 0.0
            ).astype(BF16)

    def permute_rows():
        per = head_out.shape[0]
        for g in range(NX):
            shape = (part.shape[1], rws.shape[0])
            to = lax.broadcasted_iota(jnp.int32, shape, 0)
            come = lax.broadcasted_iota(jnp.int32, shape, 1)
            source = (to // per) * (NX * per) + g * per + to % per
            pick = jnp.where(come == source, 1.0, 0.0).astype(BF16)
            rws_p[g * shape[0] : (g + 1) * shape[0], :] = dot(pick, rws[...]).astype(BF16)

    def own_band(step):
        acc[...] = dot(dense[:, rows : 2 * rows], win[step, rows : 2 * rows, :])

    def halo_side(step, side):
        halo_finish(step, side)
        first = jnp.where(first_col, 2 * rows * (1 - side), 2 * rows * side)
        at = pl.ds(pl.multiple_of(first, rows), rows)
        return dot(dense[:, at], win[step, at, :])

    def state(step, along_x):
        acc[...] += head_band(step, along_x)
        scale = jnp.concatenate([bscale[...], bscale[...]], axis=1)
        return jnp.maximum((acc[...] + halo_side(step, 1)) * scale, 0.0)

    heads_f = spread_f(hf)
    own0, over0 = gather_start(0, CHUNKS)
    load_r.wait()
    x0 = head_partial(0, rws)
    for copy in load_small:
        copy.wait()
    tabled = tables()
    for copy in heads_f:
        copy.wait_recv()
    load_w0.wait()
    width = hf.shape[-1]
    own_rows = sum(
        dot(hf[f].astype(BF16), wts[0, f * width : (f + 1) * width, :]) for f in range(NL * NC)
    )
    h4[x] = own_rows[:, :half]
    half4[z] = own_rows[:, half:]
    heads_x = group(h4.at[pl.ds(0, NX - 1)], [(h4.at[x], h4.at[x], x_peers[k]) for k in x_order])
    second = group(
        half4.at[pl.ds(0, NZ - 1)], [(half4.at[z], half4.at[z], z_peers[k]) for k in z_order]
    )
    hand0, halo0 = [], []

    def mix_next(step, over, hand, halo):
        if len(hand) < CHUNKS:
            hand.append(hand_on(step, over, len(hand)))
        hand[len(halo)].wait_recv()
        halo.append(mix(step, len(halo)))

    cross_on()
    hand0.append(hand_on(0, over0, 0))
    own0.wait_recv()
    mix_next(0, over0, hand0, halo0)
    mix_next(0, over0, hand0, halo0)
    mix_next(0, over0, hand0, halo0)
    for copy in heads_x:
        copy.wait_recv()
    along_y = spread_y(jnp.concatenate([h4[k] for k in range(NX)], axis=0))
    mix_next(0, over0, hand0, halo0)
    mix_next(0, over0, hand0, halo0)
    second = second_y(second)
    z0 = x_finish(0, x0)
    relay_on(halo0[0])
    mix_next(0, over0, hand0, halo0)
    relay_on(halo0[1])
    mix_next(0, over0, hand0, halo0)
    relay_on(halo0[2])
    mix_next(0, over0, hand0, halo0)
    load_t.wait()
    tabled.wait()
    build()
    relay_on(halo0[4])
    hand_y(along_y)
    edges()
    own_band(0)
    second = second_x(0, second)
    y0 = z_finish(0, z0)
    load_c.wait()
    for i in range(tile_rows):
        mask_cols(i)
    permute_cols()
    permute_rows()
    hscale[...] = lax.rsqrt(down_rows(hdeg[pl.ds(x, 1), :].astype(F32)))
    h_scale = hscale[pl.ds(pl.multiple_of(z * piece, piece), piece), :]
    h_scale = jnp.concatenate([h_scale, h_scale], axis=1)
    acc[...] += halo_side(0, 0)
    gath[1, pl.ds(me_f, 1)] = state(0, second).astype(BF16)[None]
    feat_b = feat_start(0, y_finish(0, y0))
    own1, over1 = gather_start(1, CHUNKS)
    x1 = head_partial(1, rws_p)
    load_w1.wait()
    hand1, halo1 = [hand_on(1, over1, 0)], []
    own1.wait_recv()
    mix_next(1, over1, hand1, halo1)
    h1 = jnp.maximum(feat_finish(0, 0, feat_b) * h_scale, 0.0)
    feat_c = feat_start(1, h1)
    mix_next(1, over1, hand1, halo1)
    z1 = x_finish(1, x1)
    for _i in range(3):
        mix_next(1, over1, hand1, halo1)
    along_x, second = spread_x(feat_finish(1, 1, feat_c))
    mix_next(1, over1, hand1, halo1)
    relay_on(halo1[0])
    mix_next(1, over1, hand1, halo1)
    relay_on(halo1[1])
    mix_next(1, over1, hand1, halo1)
    relay_on(halo1[2])
    y1 = z_finish(1, z1)
    relay_on(halo1[4])
    hand_x(along_x)
    second = second_x(1, second)
    own_band(1)
    acc[...] += halo_side(1, 0)
    feat_d = last_start(y_finish(1, y1))
    band_out[...] = state(1, second)
    sums = last_finish(feat_d)
    per = head_out.shape[0]
    near_z = hscale.shape[0] // (per * NX * NY)
    hscale[...] = lax.rsqrt(down_rows(hdeg[pl.ds(z // near_z, 1), :].astype(F32)))
    at = pl.multiple_of((z % near_z) * NY * NX * per + yh * NX * per, NX * per)
    near = hscale[pl.ds(at, NX * per), :]
    near = jnp.concatenate([near, near], axis=1)
    own_scale = jnp.zeros(head_out.shape, F32)
    for k in range(NX):
        own_scale = own_scale + jnp.where(x == k, near[k * per : (k + 1) * per, :], 0.0)
    head_out[...] = jnp.maximum(sums * own_scale, 0.0)

    for whole in ends + [all_z(0), all_z(1)]:
        whole.wait_send()
    via_sent()
    halo_sent(0)
    halo_sent(1)
    assert (n_send[0], n_recv[0]) == (N_SEND, N_RECV), (n_send, n_recv)


def write_out(band, head, band_out, head_out, sem):
    copies = [
        pltpu.make_async_copy(src, dst, sem.at[i])
        for i, (src, dst) in enumerate(((band, band_out), (head, head_out)))
    ]
    for copy in copies:
        copy.start()
    for copy in copies:
        copy.wait()


N_SEND, N_RECV = 33, 71


def body(
    band_feats,
    head_feats,
    mix_weights,
    tile_place,
    tile_vals,
    arrow_cols,
    arrow_reach,
    arrow_rows,
    band_degree,
    head_degree,
):
    rows, width = band_feats.shape
    heads = arrow_rows.shape[0]
    piece = heads // (NZ * NX)
    vmem = pl.BlockSpec(memory_space=pltpu.VMEM)
    hbm = pl.BlockSpec(memory_space=pl.ANY)
    results = pl.pallas_call(
        kernel,
        out_shape=(pltpu.VMEM((rows, width), F32), pltpu.VMEM(head_feats.shape, F32)),
        in_specs=[hbm] * 10,
        out_specs=(vmem, vmem),
        scratch_shapes=[
            pltpu.VMEM(tile_place.shape[::-1], jnp.int32),
            pltpu.VMEM((rows // TILE, TILE), jnp.int32),
            pltpu.VMEM((heads // TILE, TILE), jnp.int32),
            pltpu.VMEM((rows // TILE, TILE), jnp.int32),
            pltpu.VMEM((rows, width), F32),
            pltpu.VMEM(mix_weights.shape, BF16),
            pltpu.VMEM((tile_vals.shape[0] + 1, TILE, TILE), BF16),
            pltpu.VMEM(arrow_cols.shape, BF16),
            pltpu.VMEM(arrow_rows.shape, BF16),
            pltpu.VMEM(arrow_rows.shape, BF16),
            pltpu.VMEM((rows, 3 * rows), BF16),
            pltpu.VMEM((2, NL * NC, rows, width), BF16),
            pltpu.VMEM((2, 3 * rows, width), BF16),
            pltpu.VMEM((rows, width), F32),
            pltpu.VMEM((NX, heads // NX, width), F32),
            pltpu.VMEM((2, NX, heads // NX, width), BF16),
            pltpu.VMEM((2, NX - 1, heads // NX, width), BF16),
            pltpu.VMEM((2, NZ, piece, width), BF16),
            pltpu.VMEM((2, NZ - 1, piece, width), BF16),
            pltpu.VMEM((piece, width), BF16),
            pltpu.VMEM((NY - 1, piece, width), BF16),
            pltpu.VMEM((NY, *head_feats.shape), F32),
            pltpu.VMEM((NY - 1, *head_feats.shape), F32),
            pltpu.VMEM((NL * NC, *head_feats.shape), F32),
            pltpu.VMEM((2, NL * NC, piece, width), BF16),
            pltpu.VMEM((NL * NC, *head_feats.shape), F32),
            pltpu.VMEM((NX, head_feats.shape[0], width // 2), F32),
            pltpu.VMEM((2, len(RELAYED), rows // CHUNKS, width), BF16),
            pltpu.VMEM((len(VIA), rows // CHUNKS, width), BF16),
            pltpu.VMEM((2, NZ, NX, piece, width // 2), BF16),
            pltpu.VMEM((NZ, head_feats.shape[0], width // 2), F32),
            pltpu.VMEM((2, NX, heads // NX, width // 2), BF16),
            pltpu.VMEM(arrow_cols.shape, BF16),
            pltpu.VMEM((heads // NX, TILE), F32),
            pltpu.VMEM((rows, TILE), F32),
            pltpu.VMEM((8, TILE), jnp.int32),
            pltpu.SMEM((8, TILE), jnp.int32),
            pltpu.SemaphoreType.DMA((16,)),
            pltpu.SemaphoreType.DMA((N_SEND,)),
            pltpu.SemaphoreType.DMA((N_RECV,)),
        ],
        compiler_params=pltpu.CompilerParams(collective_id=0, has_side_effects=True),
    )(
        tile_place.T,
        band_degree.reshape(-1, TILE),
        head_degree.reshape(-1, TILE),
        arrow_reach.reshape(-1, TILE),
        band_feats,
        head_feats,
        mix_weights,
        tile_vals,
        arrow_cols,
        arrow_rows,
    )
    return pl.pallas_call(
        write_out,
        out_shape=(
            jax.ShapeDtypeStruct((rows, width), F32),
            jax.ShapeDtypeStruct(head_feats.shape, F32),
        ),
        in_specs=[vmem, vmem],
        out_specs=(hbm, hbm),
        scratch_shapes=[pltpu.SemaphoreType.DMA((2,))],
    )(*(pltpu.with_memory_space_constraint(r, pltpu.VMEM) for r in results))


def solution(mesh):
    split = Mesh(
        mesh.devices.reshape(NZ, NY, NX, NL, NC), (*ROWS, *FEAT)
    )
    return jax.shard_map(
        body,
        mesh=split,
        in_specs=(
            P(ROWS, FEAT),
            P(ROWS, FEAT),
            P(None, None, FEAT),
            P(ROWS, None),
            P(ROWS, None, None),
            P(ROWS, None),
            P(ROWS),
            P(None, ROWS),
            P(ROWS),
            P(),
        ),
        out_specs=(P(ROWS, FEAT), P(ROWS, FEAT)),
        check_vma=False,
    )
```
